256 devices in a mesh: seq: 32 (over z, y), mp: 8 (over x, core).
Axes of the slice: x: 4, y: 4, z: 8, core: 2. Of those that a mesh axis runs over, the one named last changes fastest.
Arguments:
- scored_token_targets: int32 [8192], P('seq'), may hold values from 0 to 15999
- valid: int32 [8192], P('seq'), may hold values 0 or 1
- lengths: int32 [48], replicated, may hold values from 1 to 1024, 8192 in all
- owners: int32 [48], replicated, may hold values from 0 to 31
- holders: int32 [48], replicated, may hold values from -1 to 31, as said below
- mixer_input_x: bfloat16 [2, 8192, 3584], P(None, 'seq', 'mp'), may hold values from -6 to 6
- mixer_gate_input: bfloat16 [2, 8192, 3584], P(None, 'seq', 'mp'), may hold values from -6 to 6
- input_projection_b: bfloat16 [2, 8192, 64], P(None, 'seq'), may hold values from -2.390625 to 2.390625
- output_projection_c: bfloat16 [2, 8192, 64], P(None, 'seq'), may hold values from -2.390625 to 2.390625
- token_step_sizes: float32 [2, 8192, 56], P(None, 'seq', 'mp'), may hold values from 0.01 to 0.3
- head_decay_rate: float32 [2, 56], P(None, 'mp'), may hold values from 0.0002 to 1
- head_skip_scale: float32 [2, 56], P(None, 'mp'), may hold values from 0.5 to 1.5
- prompt_held_states: bfloat16 [2, 32, 56, 64, 64], P(None, 'seq', 'mp'), may hold values from -6 to 6
- shared_output_weight: bfloat16 [3584, 3584], P('mp'), may hold values from -0.09375 to 0.09375
- adapter_down_weight: bfloat16 [3584, 128], P('mp'), may hold values from -0.09375 to 0.09375
- adapter_up_weight: bfloat16 [128, 3584], replicated, may hold values from -0.5 to 0.5
- residual: bfloat16 [8192, 2, 3584], P('seq'), may hold values from -16 to 16
- final_norm_scale: float32 [3584], replicated, may hold values from 0.5 to 1.5
- vocab_head_weight: bfloat16 [3584, 16000], P('seq', 'mp'), may hold values from -8 to 8
Outputs:
- owner_sums: float32 [32, 48], P('seq')
- token_delta: float32 [8192], P('seq')
The draws below stay inside these ranges and needn't reach their ends.
Inputs may be any that keep to these rules, and one draw needn't show every extreme that they name: `holders`: exactly 24 rollouts continue a prompt state; the others start from zeros.
All inputs are finite; a program needn't handle non-finite values. No bound on the sum of `valid` on one device may be relied on, other than what follows from the above.
Results may differ from the reference program's by a relative error of at most 0.035.
Values may be sent and summed in bfloat16 or wider, within the bound.
A program may use at most 128 MiB of HBM per device.

```python
import math
import jax
import jax.numpy as jnp
import numpy as np
from jax import lax

MODEL_WIDTH = 3584
HEADS = 56
HEAD = 64
STATE = 64
VOCAB = 16000
ADAPTER_RANK = 128
ROLLOUTS = 48
MIXER_WIDTH = 3584
TOKENS = 8192
LEN_MOST = 1024
N_SEQ = 32
N_MP = 8


def draw_holders(key, part):
    order_key = jax.random.fold_in(key, 11)
    source_key = jax.random.fold_in(key, 12)
    order = jax.random.permutation(order_key, ROLLOUTS)
    source = jax.random.randint(source_key, (ROLLOUTS,), 0, N_SEQ)
    source = jnp.where(order == 0, N_SEQ - 1, source)
    return jnp.where(order < ROLLOUTS // 2, source, -1).astype(jnp.int32)


def drawn_parts(key):
    base_key = jax.random.fold_in(key, 31)
    signs = jax.random.randint(jax.random.fold_in(base_key, 1), (4, MODEL_WIDTH), 0, 2).astype(jnp.float32) * 2.0 - 1.0
    rows_picked = jax.random.randint(jax.random.fold_in(base_key, 2), (16,), 0, TOKENS)
    cols_picked = jax.random.permutation(jax.random.fold_in(base_key, 3), VOCAB)[:8]
    return (signs, rows_picked, cols_picked)


def draw_residual(key, part):
    signs, rows_picked, cols_picked = drawn_parts(key)
    noise_key = jax.random.fold_in(key, 41)
    noise = jnp.clip(jax.random.normal(noise_key, (TOKENS, 2, MODEL_WIDTH), jnp.float32), -6.0, 6.0)
    row_dir = jnp.full((TOKENS,), -1, jnp.int32).at[rows_picked].set(jnp.arange(16, dtype=jnp.int32) % 4)
    picked = jnp.take(signs, jnp.maximum(row_dir, 0), axis=0)
    return jnp.where((row_dir >= 0)[:, None, None], noise + 8.0 * picked[:, None, :], noise).astype(jnp.bfloat16)


def draw_vocab_head_weight(key, part):
    signs, rows_picked, cols_picked = drawn_parts(key)
    noise_key = jax.random.fold_in(key, 42)
    spread = (MODEL_WIDTH // 9) ** (-0.5)
    noise = jnp.clip(jax.random.normal(noise_key, (MODEL_WIDTH, VOCAB), jnp.float32), -6.0, 6.0) * spread
    strengths = jnp.array([120.0, 180.0, 260.0, 340.0], jnp.float32)
    index = jnp.arange(8, dtype=jnp.int32)
    which = index // 2
    power = strengths[which]
    factor = power / MODEL_WIDTH * jnp.where(index % 2 == 1, 1.0 - 2.0 / power, 1.0)
    columns = jnp.transpose(jnp.take(signs, which, axis=0)) * factor[None, :]
    return noise.at[:, cols_picked].set(columns).astype(jnp.bfloat16)


def plant(values, own_key, low, largest):
    longest = values.shape.index(max(values.shape))
    spots = []
    for shift in (0, 1):
        where = [jax.random.randint(jax.random.fold_in(own_key, axis), (), 0, length) for axis, length in enumerate(values.shape)]
        where[longest] = (where[longest] + shift) % values.shape[longest]
        spots.append(tuple(where))
    return values.at[spots[0]].set(low).at[spots[1]].set(largest)


def steps_of(key, dims, cuts, least, high):
    gain, own = 1.0, jax.random.fold_in(key, 6)
    for dim, blocks in cuts:
        steps = jnp.exp(jax.random.uniform(jax.random.fold_in(own, dim), (blocks,), jnp.float32, least / len(cuts), high / len(cuts)))
        gain = gain * jnp.repeat(steps, dims[dim] // blocks).reshape([-1 if axis == dim else 1 for axis in range(len(dims))])
    return gain


def cumulative_ranks(number_of, lean):
    weights = [(1 << 20) // math.isqrt(rank ** lean) + 1 for rank in range(1, number_of + 1)]
    scale = 1 + sum(weights) // (1 << 30)
    return np.cumsum(np.array([max(1, weight // scale) for weight in weights]))


def ranked(stream_key, dims, amount, slope):
    grid = cumulative_ranks(amount, slope)
    lot = jax.random.randint(jax.random.fold_in(stream_key, 1), dims, 0, int(grid[amount - 1]))
    standing = jnp.searchsorted(jnp.asarray(grid, jnp.int32), lot, side="right")
    return jax.random.permutation(jax.random.fold_in(stream_key, 2), amount)[standing].astype(jnp.int32)


def profile(amount, total, most, slope):
    weights = [(1 << 20) // math.isqrt(standing ** slope) + 1 for standing in range(2, amount + 1)]
    spare, given = total - most - (amount - 1), [1] * (amount - 1)
    while spare > 0:
        candidates = [i for i in range(amount - 1) if given[i] < most]
        mass, remaining = sum([weights[i] for i in candidates]), spare
        for i in candidates:
            extra = min(most - given[i], max(1, remaining * weights[i] // mass), spare)
            given[i] = given[i] + extra
            spare = spare - extra
    return np.array([most] + given)


def ragged_sizes(stream_key, number_of, total, limit, slope):
    if number_of == 2:
        one = jax.random.randint(stream_key, (), max(1, total - limit), min(limit, total - 1) + 1)
        return jnp.stack([one, total - one])
    sizes = jnp.asarray(profile(number_of, total, limit, slope), jnp.int32)
    couples = (number_of - 1) // 2
    source_of, taker = sizes[1:1 + 2 * couples:2], sizes[2:2 + 2 * couples:2]
    margin = jnp.minimum(source_of - 1, limit - taker)
    shifted = jax.random.randint(jax.random.fold_in(stream_key, 1), (couples,), 0, 1 << 20) % (margin + 1)
    sizes = sizes.at[1:1 + 2 * couples:2].set(source_of - shifted).at[2:2 + 2 * couples:2].set(taker + shifted)
    return sizes[jax.random.permutation(jax.random.fold_in(stream_key, 2), number_of)]


def scatter_about(key, shape, scale, most, split=(), held_as=jnp.bfloat16):
    gain = steps_of(key, shape, split, -0.22, 0.18) if split else 1.0
    values = jax.random.normal(key, shape, jnp.float32) * scale * gain
    return jnp.minimum(jnp.maximum(values, -most), most).astype(held_as)


def setup_inputs(seed: int = 0) -> dict:
    seeds = jax.random.split(jax.random.key(seed), 20)
    return {
        "scored_token_targets": plant(ranked(seeds[0], (TOKENS,), VOCAB, 2), jax.random.fold_in(seeds[0], 3), 0, VOCAB - 1).astype(jnp.int32),
        "valid": plant((jax.random.randint(seeds[1], (TOKENS,), 0, 8) < 7).astype(jnp.int32), jax.random.fold_in(seeds[1], 1), 0, 1),
        "lengths": ragged_sizes(seeds[2], ROLLOUTS, TOKENS, LEN_MOST, 2).astype(jnp.int32),
        "owners": plant(jax.random.randint(seeds[3], (ROLLOUTS,), 0, N_SEQ), jax.random.fold_in(seeds[3], 1), 0, N_SEQ - 1).astype(jnp.int32),
        "holders": draw_holders(jax.random.fold_in(seeds[19], 71), 0),
        "mixer_input_x": scatter_about(seeds[5], (2, TOKENS, MIXER_WIDTH), 1.0, 6.0, ((1, 32), (2, 8))),
        "mixer_gate_input": scatter_about(seeds[6], (2, TOKENS, MIXER_WIDTH), 1.0, 6.0, ((1, 32), (2, 8))),
        "input_projection_b": scatter_about(seeds[7], (2, TOKENS, STATE), 0.4, 2.390625, ((1, 32),)),
        "output_projection_c": scatter_about(seeds[8], (2, TOKENS, STATE), 0.4, 2.390625, ((1, 32),)),
        "token_step_sizes": jnp.clip(jnp.exp(math.log(0.3) - 3.4011974 * jax.random.uniform(seeds[9], (2, TOKENS, HEADS), jnp.float32) ** steps_of(seeds[9], (2, TOKENS, HEADS), ((1, 32), (2, 8)), -0.2, 0.2)), 0.01, 0.3),
        "head_decay_rate": jnp.clip(jnp.exp(math.log(1.0) - 8.517193 * jax.random.uniform(seeds[10], (2, HEADS), jnp.float32) ** steps_of(seeds[10], (2, HEADS), ((1, 8),), -0.2, 0.2)), 0.0002, 1.0),
        "head_skip_scale": jnp.clip(0.5 + 1.0 * jax.random.uniform(seeds[11], (2, HEADS), jnp.float32) ** steps_of(seeds[11], (2, HEADS), ((1, 8),), -0.2, 0.2), 0.5, 1.5),
        "prompt_held_states": scatter_about(seeds[12], (2, N_SEQ, HEADS, HEAD, STATE), 1.0, 6.0, ((1, 32), (2, 8))),
        "shared_output_weight": scatter_about(seeds[13], (MIXER_WIDTH, MODEL_WIDTH), MIXER_WIDTH ** -0.5, 0.09375, ((0, 8),)),
        "adapter_down_weight": scatter_about(seeds[14], (MIXER_WIDTH, ADAPTER_RANK), MIXER_WIDTH ** -0.5, 0.09375, ((0, 8),)),
        "adapter_up_weight": scatter_about(seeds[15], (ADAPTER_RANK, MODEL_WIDTH), ADAPTER_RANK ** -0.5, 0.5),
        "residual": draw_residual(jax.random.fold_in(seeds[19], 71), 0),
        "final_norm_scale": jnp.clip(1.0 + 0.1 * jax.random.normal(seeds[17], (MODEL_WIDTH,), jnp.float32), 0.5, 1.5),
        "vocab_head_weight": draw_vocab_head_weight(jax.random.fold_in(seeds[19], 71), 0),
    }


highest = lax.Precision.HIGHEST

def root_norm(hidden, final_norm_scale):
    mean_sq = lax.optimization_barrier(jnp.mean(hidden * hidden, axis=-1, keepdims=True))
    return (hidden * lax.rsqrt(mean_sq + 1e-05) * final_norm_scale).astype(jnp.bfloat16)

def reference(scored_token_targets, valid, lengths, owners, holders, mixer_input_x, mixer_gate_input, input_projection_b, output_projection_c, token_step_sizes, head_decay_rate, head_skip_scale, prompt_held_states, shared_output_weight, adapter_down_weight, adapter_up_weight, residual, final_norm_scale, vocab_head_weight):
    position = jnp.arange(TOKENS, dtype=jnp.int32)
    starts = (jnp.cumsum(lengths) - lengths).astype(jnp.int32)
    rollout = (lax.optimization_barrier(jnp.sum((starts[None, :] <= position[:, None]).astype(jnp.int32), axis=1)) - 1).astype(jnp.int32)
    is_start = jnp.take(starts, rollout) == position
    holder_tok = jnp.take(holders, rollout).astype(jnp.int32)
    neg_rates = -head_decay_rate.astype(jnp.float32)
    x_values = jnp.transpose(mixer_input_x.astype(jnp.float32).reshape(2, TOKENS, HEADS, HEAD), (1, 0, 2, 3))
    b_values = jnp.transpose(input_projection_b.astype(jnp.float32), (1, 0, 2))
    c_values = jnp.transpose(output_projection_c.astype(jnp.float32), (1, 0, 2))
    dt_values = jnp.transpose(token_step_sizes.astype(jnp.float32), (1, 0, 2))

    def advance(state, inputs):
        x_now, b_now, c_now, dt_now, start_now, hold_now = inputs
        prompt = lax.dynamic_index_in_dim(prompt_held_states, jnp.maximum(hold_now, 0), axis=1, keepdims=False).astype(jnp.float32)
        prompt = jnp.where(hold_now >= 0, prompt, jnp.zeros_like(prompt))
        state = jnp.where(start_now, prompt, state)
        factor = jnp.exp(dt_now * neg_rates)
        state = factor[:, :, None, None] * state + (dt_now[:, :, None] * x_now)[:, :, :, None] * b_now[:, None, None, :]
        y_now = jnp.einsum('mhpn,mn->mhp', state, c_now, precision=highest)
        return (state, y_now)
    state_zero = jnp.zeros((2, HEADS, HEAD, STATE), jnp.float32)
    final_state, y_values = lax.scan(advance, state_zero, (x_values, b_values, c_values, dt_values, is_start, holder_tok))
    y_values = y_values + head_skip_scale.astype(jnp.float32)[None, :, :, None] * x_values
    y_values = y_values.reshape(TOKENS, 2, MIXER_WIDTH)
    gate_values = jnp.transpose(mixer_gate_input.astype(jnp.float32), (1, 0, 2))
    gated_output = (y_values * jax.nn.silu(gate_values)).astype(jnp.bfloat16)
    layer_width = MIXER_WIDTH // N_MP

    def add_block(holder_index, running):
        part_rows = lax.dynamic_slice_in_dim(gated_output, holder_index * layer_width, layer_width, 2)
        weight_rows = lax.dynamic_slice_in_dim(shared_output_weight, holder_index * layer_width, layer_width, 0)
        adapter_down_rows = lax.dynamic_slice_in_dim(adapter_down_weight, holder_index * layer_width, layer_width, 0)
        base_output = jnp.einsum('tmi,id->tmd', part_rows.astype(jnp.float32), weight_rows.astype(jnp.float32))
        low_rank_rows = jnp.dot(part_rows[:, 0], adapter_down_rows, preferred_element_type=jnp.float32).astype(jnp.bfloat16)
        adapter_output = jnp.dot(low_rank_rows, adapter_up_weight, preferred_element_type=jnp.float32)
        adapter_term_rows = jnp.stack([base_output[:, 0] + adapter_output, base_output[:, 1]], axis=1).astype(jnp.bfloat16)
        adapter_term_rows = lax.optimization_barrier(adapter_term_rows)
        return running + adapter_term_rows.astype(jnp.float32)
    mixed = lax.fori_loop(0, N_MP, add_block, jnp.zeros((TOKENS, 2, MODEL_WIDTH), jnp.float32))
    normed = root_norm(residual.astype(jnp.float32) + mixed, final_norm_scale)
    logprobs = []
    for model_index in range(2):
        logits = jnp.dot(normed[:, model_index], vocab_head_weight, preferred_element_type=jnp.float32)
        vocab_top = lax.optimization_barrier(jnp.max(logits, axis=1))
        vocab_total = lax.optimization_barrier(jnp.sum(jnp.exp(logits - vocab_top[:, None]), axis=1))
        target_logit = jnp.take_along_axis(logits, scored_token_targets[:, None].astype(jnp.int32), axis=1)[:, 0]
        logprobs.append(target_logit - vocab_top - jnp.log(vocab_total))
    token_delta = (logprobs[0] - logprobs[1]) * valid.astype(jnp.float32)
    member_table = (rollout[:, None] == jnp.arange(ROLLOUTS, dtype=jnp.int32)[None, :]).astype(jnp.float32)
    roll_sums = jnp.dot(token_delta, member_table, precision=highest) / lengths.astype(jnp.float32)
    owner_table = (owners[None, :] == jnp.arange(N_SEQ, dtype=jnp.int32)[:, None]).astype(jnp.float32)
    owner_sums = owner_table * roll_sums[None, :]
    return (owner_sums, token_delta)
```

```python
import functools

import jax
import jax.numpy as jnp
from jax import lax
from jax.experimental import pallas as pl
from jax.experimental.pallas import tpu as pltpu
from jax.sharding import PartitionSpec as P

HIGHEST = lax.Precision.HIGHEST
MESH = pl.DeviceIdType.MESH
Y, Z = 4, 8
X, CORES = 4, 2
REACH = 4
VMEM_BYTES = 56 * 1024 * 1024
LOW = -1e30


def iota(shape, dim):
    return lax.broadcasted_iota(jnp.int32, shape, dim)


def rollout_tables(len_row, first_row, tok):
    lanes = len_row.shape[1]
    row_i, col_i = iota((lanes, lanes), 0), iota((lanes, lanes), 1)
    table = jnp.broadcast_to(len_row, (lanes, lanes))
    starts_col = jnp.sum(jnp.where(col_i < row_i, table, 0.0), axis=1, keepdims=True)
    len_col = jnp.sum(jnp.where(col_i == row_i, table, 0.0), axis=1, keepdims=True)
    starts_row = jnp.sum(jnp.where(row_i < col_i, len_col, 0.0), axis=0, keepdims=True)
    first = jnp.float32(1) * first_row
    pos_col = iota((tok, lanes), 0).astype(jnp.float32) + first
    pos_row = iota((lanes, tok), 1).astype(jnp.float32) + first
    roll_col = jnp.sum(jnp.where(starts_row <= pos_col, 1.0, 0.0), axis=1, keepdims=True) - 1.0
    roll_row = jnp.sum(jnp.where(starts_col <= pos_row, 1.0, 0.0), axis=0, keepdims=True) - 1.0
    return starts_row, roll_col, roll_row, pos_col


def spread(values, heads, inner):
    pick = (iota((heads, inner), 1) // (inner // heads) == iota((heads, inner), 0)).astype(jnp.float32)
    return jnp.dot(values, pick, precision=HIGHEST, preferred_element_type=jnp.float32)


def local_mix_kernel(len_ref, x_ref, b_ref, c_ref, dt_ref, rate_ref, skip_ref, y_ref, dec_ref, e_ref, dl_ref):
    models, tok, inner = x_ref.shape
    heads = dt_ref.shape[2]
    head = inner // heads
    first_row = lax.axis_index("seq") * tok
    _, roll_col, roll_row, _ = rollout_tables(len_ref[...].astype(jnp.float32), first_row, tok)
    t_i, s_i = iota((tok, tok), 0), iota((tok, tok), 1)
    mask = (roll_col == roll_row) & (s_i <= t_i)
    mask_f = mask.astype(jnp.float32)
    tail = roll_col == roll_col[tok - 1 : tok, :]
    eye = (iota((heads, heads), 0) == iota((heads, heads), 1)).astype(jnp.float32)
    for m in range(models):
        dt = dt_ref[m]
        run = jnp.dot(mask_f, -dt * rate_ref[m : m + 1, :], precision=HIGHEST, preferred_element_type=jnp.float32)
        up = jnp.log(dt) - run
        up_rows = lax.dot_general(
            eye, up, (((1,), (1,)), ((), ())), precision=HIGHEST, preferred_element_type=jnp.float32
        )
        gram = lax.dot_general(
            c_ref[m], b_ref[m], (((1,), (1,)), ((), ())), preferred_element_type=jnp.float32
        )
        x_f = x_ref[m].astype(jnp.float32)
        pair = 2 * head
        skips = spread(jnp.broadcast_to(skip_ref[m : m + 1, :], (8, heads)), heads, inner)[0:1]
        for lo in range(0, inner, pair):
            width = min(pair, inner - lo)
            x_pair = x_ref[m, :, lo : lo + width]
            outs = []
            for h in range(lo // head, (lo + width) // head):
                gap = jnp.where(mask, run[:, h : h + 1] + up_rows[h : h + 1, :], LOW)
                weights = (jnp.exp(gap) * gram).astype(jnp.bfloat16)
                outs.append(jnp.dot(weights, x_pair, preferred_element_type=jnp.float32))
            part = outs[0]
            if len(outs) == 2:
                part = jnp.where(iota((tok, width), 1) < head, outs[0], outs[1])
            y_ref[m, :, lo : lo + width] = part + skips[:, lo : lo + width] * x_f[:, lo : lo + width]
        last = run[tok - 1 : tok, :]
        end_w = jnp.where(tail, jnp.exp(jnp.where(tail, last + up, LOW)), 0.0)
        x_end = (x_f * spread(end_w, heads, inner)).astype(jnp.bfloat16)
        e_ref[m] = lax.dot_general(
            b_ref[m], x_end, (((0,), (0,)), ((), ())), preferred_element_type=jnp.float32
        ).astype(jnp.bfloat16)
        dl_ref[m] = spread(jnp.broadcast_to(last, (8, heads)), heads, inner)
        dec_ref[m] = spread(jnp.exp(run), heads, inner)


def vmem():
    return pl.BlockSpec(memory_space=pltpu.VMEM)


def anywhere():
    return pl.BlockSpec(memory_space=pl.ANY)


def smem():
    return pl.BlockSpec(memory_space=pltpu.SMEM)


def local_mix(len_row, x, b, c, dt, rate, skip):
    models, tok, inner = x.shape
    state = b.shape[2]
    return pl.pallas_call(
        local_mix_kernel,
        out_shape=(
            jax.ShapeDtypeStruct((models, tok, inner), jnp.float32),
            jax.ShapeDtypeStruct((models, tok, inner), jnp.float32),
            jax.ShapeDtypeStruct((models, state, inner), jnp.bfloat16),
            jax.ShapeDtypeStruct((models, 8, inner), jnp.float32),
        ),
        in_specs=[vmem()] * 7,
        out_specs=(vmem(),) * 4,
        compiler_params=pltpu.CompilerParams(vmem_limit_bytes=VMEM_BYTES),
        cost_estimate=pl.CostEstimate(flops=2 * 10**9, bytes_accessed=4 * 10**6, transcendentals=10**6),
        name="local_mix",
    )(len_row, x, b, c, dt, rate, skip)


def greet(barrier, peers):
    for peer in peers:
        pl.semaphore_signal(barrier, inc=1, device_id=peer, device_id_type=MESH)
    pl.semaphore_wait(barrier, len(peers))


def states_kernel(
    pt_ref, e_ref, dl_ref, wo_ref, dw_ref,
    pall_ref, en_ref, dn_ref, wos_ref, dws_ref,
    send_sem, recv_sem, send2, recv2, own_sem,
):
    seq, mp = lax.axis_index("seq"), lax.axis_index("mp")
    z, y = seq // Y, lax.rem(seq, Y)
    count = Y * Z

    def at_y(d):
        return (z * Y + lax.rem(y + d + Y, Y), mp)

    def at_z(d):
        return (lax.rem(z + d + Z, Z) * Y + y, mp)

    def at_s(d):
        return (lax.rem(seq + d + count, count), mp)

    sibling = (seq, mp + 1 - 2 * lax.rem(mp, CORES))
    greet(
        pltpu.get_barrier_semaphore(),
        [at_y(1), at_y(-1), at_y(2), at_z(1), at_z(-1), sibling]
        + [at_s(d) for d in range(1, REACH + 1)]
        + [at_s(-d) for d in range(1, REACH + 1)],
    )
    slot = [0]

    def send(src, dst, peer):
        k = slot[0]
        slot[0] += 1
        copy = pltpu.make_async_remote_copy(
            src_ref=src, dst_ref=dst, send_sem=send_sem.at[k], recv_sem=recv_sem.at[k],
            device_id=peer, device_id_type=MESH,
        )
        copy.start()
        return copy

    own = [
        pltpu.make_async_copy(pt_ref.at[m], pall_ref.at[m, z, y], own_sem.at[m]) for m in range(2)
    ]
    for copy in own:
        copy.start()
    waits = []
    a_y = [send(pt_ref.at[0], pall_ref.at[0, z, y], at_y(d)) for d in (1, -1, 2)]
    b_right = send(pt_ref.at[1], pall_ref.at[1, z, y], at_z(1))
    b_left = send(pt_ref.at[1], pall_ref.at[1, z, y], at_z(-1))
    for d in range(1, REACH + 1):
        waits.append(send(e_ref, en_ref.at[d - 1], at_s(d)))
        waits.append(send(dl_ref, dn_ref.at[d - 1], at_s(d)))
    waits.append(send(wo_ref, wos_ref, sibling))
    waits.append(send(dw_ref, dws_ref, sibling))
    for copy in own:
        copy.wait()
    for copy in a_y:
        copy.wait_recv()
    a_right = send(pall_ref.at[0, z], pall_ref.at[0, z], at_z(1))
    a_left = send(pall_ref.at[0, z], pall_ref.at[0, z], at_z(-1))
    sends = list(a_y) + [b_right, b_left, a_right, a_left]
    for k in range(1, Z // 2):
        src = lax.rem(z - k + Z, Z)
        b_right.wait_recv()
        b_right = send(pall_ref.at[1, src, y], pall_ref.at[1, src, y], at_z(1))
        sends.append(b_right)
        src = lax.rem(z + k, Z)
        b_left.wait_recv()
        if k < Z // 2 - 1:
            b_left = send(pall_ref.at[1, src, y], pall_ref.at[1, src, y], at_z(-1))
            sends.append(b_left)
    b_right.wait_recv()
    b_y = [send(pall_ref.at[1, :, y], pall_ref.at[1, :, y], at_y(d)) for d in (1, -1, 2)]
    for k in range(1, Z // 2):
        src = lax.rem(z - k + Z, Z)
        a_right.wait_recv()
        a_right = send(pall_ref.at[0, src], pall_ref.at[0, src], at_z(1))
        sends.append(a_right)
        src = lax.rem(z + k, Z)
        a_left.wait_recv()
        if k < Z // 2 - 1:
            a_left = send(pall_ref.at[0, src], pall_ref.at[0, src], at_z(-1))
            sends.append(a_left)
    a_right.wait_recv()
    for copy in b_y:
        copy.wait_recv()
    for copy in waits:
        copy.wait_recv()
    for copy in sends + b_y + waits:
        copy.wait_send()


def states(pt, e, dl, wo, dw):
    models, state, inner = pt.shape
    out = (
        jax.ShapeDtypeStruct((models, Z, Y, state, inner), pt.dtype),
        jax.ShapeDtypeStruct((REACH,) + e.shape, e.dtype),
        jax.ShapeDtypeStruct((REACH,) + dl.shape, dl.dtype),
        jax.ShapeDtypeStruct(wo.shape, wo.dtype),
        jax.ShapeDtypeStruct(dw.shape, dw.dtype),
    )
    copies = 3 + 2 * REACH + 2 + 3 + 2 * 7
    return pl.pallas_call(
        states_kernel,
        out_shape=out,
        in_specs=[anywhere()] * 5,
        out_specs=(anywhere(),) * 5,
        scratch_shapes=[
            pltpu.SemaphoreType.DMA((copies,)),
            pltpu.SemaphoreType.DMA((copies,)),
            pltpu.SemaphoreType.DMA((1,)),
            pltpu.SemaphoreType.DMA((1,)),
            pltpu.SemaphoreType.DMA((2,)),
        ],
        compiler_params=pltpu.CompilerParams(
            collective_id=1, has_side_effects=True, vmem_limit_bytes=VMEM_BYTES
        ),
        cost_estimate=pl.CostEstimate(flops=0, bytes_accessed=10**8, transcendentals=0),
        name="state_exchange",
    )(pt, e, dl, wo, dw)


def finish_mix_kernel(
    len_s, hold_s, len_ref, hold_ref, y_ref, dec_ref, c_ref, z_ref, pall_ref, en_ref, dn_ref, g_ref, acc_ref
):
    models, tok, inner = y_ref.shape
    first_row = lax.axis_index("seq") * tok
    starts_row, roll_col, _, _ = rollout_tables(len_ref[...].astype(jnp.float32), first_row, tok)
    first = jnp.float32(1) * first_row
    start0 = jnp.max(jnp.where(starts_row <= first, starts_row, -1.0), axis=1, keepdims=True)
    inherits = start0 < first
    fresh_rows = jnp.where(starts_row < first, 1.0, 0.0)
    lanes = starts_row.shape[1]
    lane_f = iota((tok, lanes), 1).astype(jnp.float32)
    inherited = jnp.sum(jnp.where(roll_col == lane_f, fresh_rows, 0.0), axis=1, keepdims=True) > 0.5

    def scan(r, carry):
        start, lo, hi, hold0 = carry
        lo = jnp.where(start < first_row, r + 1, lo)
        hi = jnp.where(start < first_row + tok, r + 1, hi)
        hold0 = jnp.where(start < first_row, hold_s[0, r], hold0)
        return start + len_s[0, r], lo, hi, hold0

    rolls = len_s.shape[1]
    _, lo, hi, hold0 = lax.fori_loop(
        0, rolls, scan, (jnp.int32(0), jnp.int32(0), jnp.int32(0), jnp.int32(-1))
    )
    hold0 = jnp.where(hold0 < 0, -1, hold0)
    source = jnp.maximum(hold0, 0)
    for m in range(models):
        total = jnp.zeros((1, inner), jnp.float32)
        arriving = jnp.zeros((c_ref.shape[2], inner), jnp.float32)
        for k in range(1, REACH + 1):
            near = start0 < first - jnp.float32((k - 1) * tok)
            arriving = arriving + jnp.where(near, jnp.exp(total) * en_ref[k - 1, m].astype(jnp.float32), 0.0)
            total = jnp.where(near, total + dn_ref[k - 1, m][0:1], total)
        begun = jnp.exp(total) * pall_ref[m, source].astype(jnp.float32)
        arriving = arriving + jnp.where(inherits & (hold0 >= 0), begun, 0.0)
        c_in = jnp.where(inherited, c_ref[m].astype(jnp.float32), 0.0).astype(jnp.bfloat16)
        high = arriving.astype(jnp.bfloat16)
        low = (arriving - high.astype(jnp.float32)).astype(jnp.bfloat16)
        acc_ref[m] = jnp.dot(c_in, high, preferred_element_type=jnp.float32) + jnp.dot(
            c_in, low, preferred_element_type=jnp.float32
        )

    def borrow(r, carry):
        held = hold_s[0, r]

        @pl.when(held >= 0)
        def _():
            mine = roll_col == r.astype(jnp.float32)
            for m in range(models):
                c_r = jnp.where(mine, c_ref[m].astype(jnp.float32), 0.0).astype(jnp.bfloat16)
                acc_ref[m] += jnp.dot(c_r, pall_ref[m, held], preferred_element_type=jnp.float32)

        return carry

    lax.fori_loop(lo, hi, borrow, 0)
    for m in range(models):
        gate = z_ref[m].astype(jnp.float32)
        out = y_ref[m] + dec_ref[m] * acc_ref[m]
        g_ref[m] = (out * (gate / (1.0 + jnp.exp(-gate)))).astype(jnp.bfloat16)


def finish_mix(len_row, hold_row, lengths, holders, y, dec, c, z, pall, en, dn):
    models, tok, inner = y.shape
    return pl.pallas_call(
        finish_mix_kernel,
        out_shape=jax.ShapeDtypeStruct((models, tok, inner), jnp.bfloat16),
        in_specs=[smem()] * 2 + [vmem()] * 9,
        out_specs=vmem(),
        scratch_shapes=[pltpu.VMEM((models, tok, inner), jnp.float32)],
        compiler_params=pltpu.CompilerParams(vmem_limit_bytes=VMEM_BYTES),
        cost_estimate=pl.CostEstimate(flops=10**9, bytes_accessed=8 * 10**6, transcendentals=10**6),
        name="finish_mix",
    )(lengths, holders, len_row, hold_row, y, dec, c, z, pall, en, dn)


def project_kernel(
    g_ref, wo_ref, wos_ref, dw_ref, dws_ref, up_ref, res_ref, scale_ref, nall_ref,
    gs_ref, low_ref, acc_ref, out_ref, in_ref, h_ref, n_ref,
    g_send, g_recv, r_send, r_recv, a_send, a_recv, f_send, f_recv, own_sem,
):
    seq, mp = lax.axis_index("seq"), lax.axis_index("mp")
    x, core = mp // CORES, lax.rem(mp, CORES)
    chunks = acc_ref.shape[0]
    width = acc_ref.shape[4]
    share = res_ref.shape[1]
    model_width = res_ref.shape[2]
    inner = g_ref.shape[4]
    rows = X * share
    sibling = (seq, x * CORES + 1 - core)

    def at_x(d):
        return (seq, lax.rem(x + d + X, X) * CORES + core)

    greet(pltpu.get_barrier_semaphore(), [sibling, at_x(1), at_x(2), at_x(3)])
    gated = pltpu.make_async_remote_copy(
        src_ref=g_ref.at[:, :, 1 - core], dst_ref=gs_ref, send_sem=g_send, recv_sem=g_recv,
        device_id=sibling, device_id_type=MESH,
    )
    gated.start()
    own_g = g_ref[:, :, core].reshape(2 * rows, inner)
    low = jnp.dot(own_g[:rows], dw_ref[...], preferred_element_type=jnp.float32)
    gated.wait_recv()
    sib_g = gs_ref[...].reshape(2 * rows, inner)
    low = low + jnp.dot(sib_g[:rows], dws_ref[...], preferred_element_type=jnp.float32)
    low_ref[...] = low.astype(jnp.bfloat16)

    def scatter(n, d):
        return pltpu.make_async_remote_copy(
            src_ref=out_ref.at[n, :, lax.rem(x + d, X)], dst_ref=in_ref.at[d - 1, n],
            send_sem=r_send.at[d - 1, n], recv_sem=r_recv.at[d - 1, n],
            device_id=at_x(d), device_id_type=MESH,
        )

    def chunk(n, carry):
        cols = pl.ds(pl.multiple_of(n * width, width), width)
        acc = jnp.dot(
            g_ref[:, :, core].reshape(2 * rows, inner), wo_ref[:, cols], preferred_element_type=jnp.float32
        ) + jnp.dot(gs_ref[...].reshape(2 * rows, inner), wos_ref[:, cols], preferred_element_type=jnp.float32)
        more = jnp.dot(low_ref[...], up_ref[:, cols], preferred_element_type=jnp.float32)
        acc_ref[n, 0] = (acc[:rows] + more).reshape(X, share, width)
        acc_ref[n, 1] = acc[rows:].reshape(X, share, width)
        out_ref[n] = acc_ref[n].astype(jnp.bfloat16)
        for d in (2, 1, 3):
            scatter(n, d).start()
        return carry

    lax.fori_loop(0, chunks, chunk, 0)

    def gather(n, square):
        cols = pl.ds(pl.multiple_of(n * width, width), width)
        total = acc_ref[n, :, x]
        for d in (1, 3, 2):
            scatter(n, d).wait_recv()
            total = total + in_ref[d - 1, n].astype(jnp.float32)
        total = total + res_ref[:, :, cols].astype(jnp.float32)
        h_ref[:, :, cols] = total
        return square + jnp.sum(total * total, axis=2, keepdims=True)

    square = lax.fori_loop(0, chunks, gather, jnp.zeros((2, share, 1), jnp.float32))
    n_ref[...] = (h_ref[...] * lax.rsqrt(square / model_width + 1e-05) * scale_ref[...]).astype(jnp.bfloat16)

    def spread_out(m, d):
        return pltpu.make_async_remote_copy(
            src_ref=n_ref.at[m], dst_ref=nall_ref.at[m, mp],
            send_sem=a_send.at[d, m], recv_sem=a_recv.at[d, m],
            device_id=sibling if d == 0 else at_x(d), device_id_type=MESH,
        )

    def forward(m, d):
        block = nall_ref.at[m, lax.rem(x - d + X, X) * CORES + core]
        return pltpu.make_async_remote_copy(
            src_ref=block, dst_ref=block, send_sem=f_send.at[d - 1, m], recv_sem=f_recv.at[d - 1, m],
            device_id=sibling, device_id_type=MESH,
        )

    for m in range(2):
        for d in (2, 1, 3, 0):
            spread_out(m, d).start()
    keep = pltpu.make_async_copy(n_ref, nall_ref.at[:, mp], own_sem)
    keep.start()
    for m in range(2):
        for d in (1, 3, 2):
            spread_out(m, d).wait_recv()
            forward(m, d).start()
    keep.wait()
    gated.wait_send()

    def drain(n, carry):
        for d in (1, 2, 3):
            scatter(n, d).wait_send()
        return carry

    lax.fori_loop(0, chunks, drain, 0)
    for m in range(2):
        spread_out(m, 0).wait_recv()
        for d in range(4):
            spread_out(m, d).wait_send()
        for d in (1, 2, 3):
            forward(m, d).wait_send()
            forward(m, d).wait_recv()


def project(gated, wo, wos, dw, dws, up, res, scale):
    models, tok, inner = gated.shape
    width_all = wo.shape[1]
    share = res.shape[1]
    width = 512
    chunks = width_all // width
    bf16, f32 = jnp.bfloat16, jnp.float32
    dma = pltpu.SemaphoreType.DMA
    return pl.pallas_call(
        project_kernel,
        out_shape=jax.ShapeDtypeStruct((models, X * CORES, share, width_all), bf16),
        in_specs=[vmem()] * 8,
        out_specs=anywhere(),
        scratch_shapes=[
            pltpu.VMEM((models, X, share, inner), bf16),
            pltpu.VMEM((X * share, dw.shape[1]), bf16),
            pltpu.VMEM((chunks, models, X, share, width), f32),
            pltpu.VMEM((chunks, models, X, share, width), bf16),
            pltpu.VMEM((X - 1, chunks, models, share, width), bf16),
            pltpu.VMEM((models, share, width_all), f32),
            pltpu.VMEM((models, share, width_all), bf16),
            dma, dma, dma((3, chunks)), dma((3, chunks)), dma((4, 2)), dma((4, 2)), dma((3, 2)), dma((3, 2)), dma,
        ],
        compiler_params=pltpu.CompilerParams(
            collective_id=2, has_side_effects=True, vmem_limit_bytes=VMEM_BYTES
        ),
        cost_estimate=pl.CostEstimate(flops=10**10, bytes_accessed=10**8, transcendentals=0),
        name="project_norm",
    )(gated.reshape(models, X, CORES, share, inner), wo, wos, dw, dws, up, res, scale)


def logits_kernel(vocab, n_ref, w_ref, tgt_ref, stat_ref, max_ref, sum_ref, hit_ref):
    step = pl.program_id(0)
    tile = w_ref.shape[1]
    rows = n_ref.shape[0]

    @pl.when(step == 0)
    def _():
        max_ref[...] = jnp.full(max_ref.shape, -3e38, jnp.float32)
        sum_ref[...] = jnp.zeros(sum_ref.shape, jnp.float32)
        hit_ref[...] = jnp.zeros(hit_ref.shape, jnp.float32)

    logits = jnp.dot(n_ref[...], w_ref[...], preferred_element_type=jnp.float32)
    col = iota((rows, tile), 1) + step * tile
    real = col < vocab
    logits = jnp.where(real, logits, -3e38)
    top = jnp.maximum(max_ref[...], jnp.max(logits, axis=1, keepdims=True))
    sum_ref[...] = sum_ref[...] * jnp.exp(max_ref[...] - top) + jnp.sum(
        jnp.where(real, jnp.exp(logits - top), 0.0), axis=1, keepdims=True
    )
    max_ref[...] = top
    hit_ref[...] += jnp.sum(jnp.where(real & (col == tgt_ref[...]), logits, 0.0), axis=1, keepdims=True)

    @pl.when(step == pl.num_programs(0) - 1)
    def _():
        lane = iota((rows, 128), 1)
        packed = jnp.where(
            lane == 0, max_ref[...], jnp.where(lane == 1, sum_ref[...], jnp.where(lane == 2, hit_ref[...], 0.0))
        )
        stat_ref[...] = jnp.transpose(packed)[0:8]


def logit_stats(normed, weight, target):
    rows, depth = normed.shape
    vocab = weight.shape[1]
    tile = 512
    return pl.pallas_call(
        functools.partial(logits_kernel, vocab),
        grid=(pl.cdiv(vocab, tile),),
        out_shape=jax.ShapeDtypeStruct((8, rows), jnp.float32),
        in_specs=[
            pl.BlockSpec((rows, depth), lambda j: (0, 0), pipeline_mode=pl.Buffered(1)),
            pl.BlockSpec((depth, tile), lambda j: (0, j)),
            pl.BlockSpec((rows, 1), lambda j: (0, 0), pipeline_mode=pl.Buffered(1)),
        ],
        out_specs=pl.BlockSpec((8, rows), lambda j: (0, 0)),
        scratch_shapes=[pltpu.VMEM((rows, 1), jnp.float32)] * 3,
        compiler_params=pltpu.CompilerParams(vmem_limit_bytes=VMEM_BYTES),
        cost_estimate=pl.CostEstimate(flops=8 * 10**9, bytes_accessed=2 * 10**7, transcendentals=10**6),
        name="logit_stats",
    )(normed, weight, target)


def deltas_kernel(
    stat_ref, valid_ref, len_ref, owner_ref, sums_ref, delta_ref,
    all_ref, part_ref, parts_ref, s_send, s_recv, p_send, p_recv,
):
    seq, mp = lax.axis_index("seq"), lax.axis_index("mp")
    peers, count = X * CORES, Y * Z
    tok = valid_ref.shape[1]
    barrier = pltpu.get_barrier_semaphore()
    for d in range(1, peers):
        pl.semaphore_signal(barrier, inc=1, device_id=(seq, lax.rem(mp + d, peers)), device_id_type=MESH)

    def hello(d, carry):
        pl.semaphore_signal(barrier, inc=1, device_id=(lax.rem(seq + d, count), mp), device_id_type=MESH)
        return carry

    lax.fori_loop(1, count, hello, 0)
    pl.semaphore_wait(barrier, peers - 1 + count - 1)

    def stats(d):
        return pltpu.make_async_remote_copy(
            src_ref=stat_ref, dst_ref=all_ref.at[mp], send_sem=s_send.at[d], recv_sem=s_recv.at[d],
            device_id=(seq, lax.rem(mp + d, peers)), device_id_type=MESH,
        )

    for d in range(1, peers):
        stats(d).start()
    all_ref[mp] = stat_ref[...]
    starts_row, roll_col, _, _ = rollout_tables(len_ref[...].astype(jnp.float32), seq * tok, tok)
    lanes = starts_row.shape[1]
    member = (roll_col == iota((tok, lanes), 1).astype(jnp.float32)).astype(jnp.float32)
    for d in range(1, peers):
        stats(d).wait_recv()
    tops = [all_ref[k][0:1] for k in range(peers)]
    top = functools.reduce(jnp.maximum, tops)
    total = functools.reduce(
        jnp.add, [all_ref[k][1:2] * jnp.exp(tops[k] - top) for k in range(peers)]
    )
    hit = functools.reduce(jnp.add, [all_ref[k][2:3] for k in range(peers)])
    logprob = hit - top - jnp.log(total)
    delta = (logprob[:, :tok] - logprob[:, tok:]) * valid_ref[...].astype(jnp.float32)
    delta_ref[...] = delta
    part_ref[...] = jnp.dot(
        jnp.broadcast_to(delta, (8, tok)), member, precision=HIGHEST, preferred_element_type=jnp.float32
    )

    def parts(d):
        return pltpu.make_async_remote_copy(
            src_ref=part_ref, dst_ref=parts_ref.at[seq], send_sem=p_send.at[d], recv_sem=p_recv.at[d],
            device_id=(lax.rem(seq + d, count), mp), device_id_type=MESH,
        )

    def begin(d, carry):
        parts(d).start()
        return carry

    def end(d, carry):
        parts(d).wait_recv()
        return carry

    def drain(d, carry):
        parts(d).wait_send()
        return carry

    lax.fori_loop(1, count, begin, 0)
    parts_ref[seq] = part_ref[...]
    lax.fori_loop(1, count, end, 0)
    sums = functools.reduce(jnp.add, [parts_ref[k] for k in range(count)])[0:1] / len_ref[...].astype(jnp.float32)
    mine = jnp.where(owner_ref[...] == seq, sums, 0.0)
    sums_ref[...] = mine[:, : sums_ref.shape[1]]
    for d in range(1, peers):
        stats(d).wait_send()
    lax.fori_loop(1, count, drain, 0)


def deltas(stat, valid_row, len_row, owner_row, rolls):
    peers, count = X * CORES, Y * Z
    tok = valid_row.shape[1]
    lanes = len_row.shape[1]
    dma = pltpu.SemaphoreType.DMA
    return pl.pallas_call(
        deltas_kernel,
        out_shape=(
            jax.ShapeDtypeStruct((1, rolls), jnp.float32),
            jax.ShapeDtypeStruct((1, tok), jnp.float32),
        ),
        in_specs=[vmem()] * 4,
        out_specs=(vmem(),) * 2,
        scratch_shapes=[
            pltpu.VMEM((peers,) + stat.shape, jnp.float32),
            pltpu.VMEM((8, lanes), jnp.float32),
            pltpu.VMEM((count, 8, lanes), jnp.float32),
            dma((peers,)), dma((peers,)), dma((count,)), dma((count,)),
        ],
        compiler_params=pltpu.CompilerParams(
            collective_id=3, has_side_effects=True, vmem_limit_bytes=VMEM_BYTES
        ),
        name="deltas",
    )(stat, valid_row, len_row, owner_row)


def shards(
    scored_token_targets, valid, lengths, owners, holders, mixer_input_x, mixer_gate_input,
    input_projection_b, output_projection_c, token_step_sizes, head_decay_rate, head_skip_scale,
    prompt_held_states, shared_output_weight, adapter_down_weight, adapter_up_weight,
    residual, final_norm_scale, vocab_head_weight,
):
    tok = scored_token_targets.shape[0]
    models, _, inner = mixer_input_x.shape
    state = input_projection_b.shape[2]
    rolls = lengths.shape[0]
    share = tok // (X * CORES)
    mp = lax.axis_index("mp")
    head_all = lax.all_gather(vocab_head_weight, "seq", axis=0, tiled=True)

    def row(values, fill):
        return jnp.pad(values, (0, 128 - rolls), constant_values=fill)[None, :]

    len_row, hold_row, owner_row = row(lengths, 0), row(holders, -1), row(owners, -1)
    prompts = jnp.transpose(prompt_held_states[:, 0], (0, 3, 1, 2)).reshape(models, state, inner)
    own_res = jnp.transpose(lax.dynamic_slice_in_dim(residual, mp * share, share, 0), (1, 0, 2))
    y, dec, ends, last = local_mix(
        len_row, mixer_input_x, input_projection_b, output_projection_c, token_step_sizes,
        head_decay_rate, head_skip_scale,
    )
    pall, en, dn, wos, dws = states(prompts, ends, last, shared_output_weight, adapter_down_weight)
    gated = finish_mix(
        len_row, hold_row, lengths[None, :], holders[None, :], y, dec, output_projection_c, mixer_gate_input,
        pall.reshape(models, Z * Y, state, inner), en, dn,
    )
    normed = project(
        gated, shared_output_weight, wos, adapter_down_weight, dws, adapter_up_weight, own_res,
        final_norm_scale[None, :],
    )
    vocab = vocab_head_weight.shape[1]
    local = scored_token_targets - mp * vocab
    target = jnp.concatenate([local, local])[:, None]
    stat = logit_stats(normed.reshape(models * tok, -1), head_all, target)
    sums, delta = deltas(stat, valid[None, :], len_row, owner_row, rolls)
    return sums, delta.reshape(tok)


def solution(mesh):
    placed = (
        P("seq"), P("seq"), P(), P(), P(),
        P(None, "seq", "mp"), P(None, "seq", "mp"),
        P(None, "seq", None), P(None, "seq", None), P(None, "seq", "mp"),
        P(None, "mp"), P(None, "mp"), P(None, "seq", "mp", None, None),
        P("mp", None), P("mp", None), P(), P("seq", None, None), P(), P("seq", "mp"),
    )
    return jax.shard_map(
        shards, mesh=mesh, in_specs=placed, out_specs=(P("seq", None), P("seq")), check_vma=False
    )
```

```python
import functools

import jax
import jax.numpy as jnp
from jax import lax
from jax.experimental import pallas as pl
from jax.experimental.pallas import tpu as pltpu
from jax.sharding import PartitionSpec as P

HIGHEST = lax.Precision.HIGHEST
MESH = pl.DeviceIdType.MESH
Y, Z = 4, 8
X, CORES = 4, 2
REACH = 4
VMEM_BYTES = 56 * 1024 * 1024
LOW = -1e30


def iota(shape, dim):
    return lax.broadcasted_iota(jnp.int32, shape, dim)


def rollout_tables(len_row, first_row, tok):
    lanes = len_row.shape[1]
    row_i, col_i = iota((lanes, lanes), 0), iota((lanes, lanes), 1)
    table = jnp.broadcast_to(len_row, (lanes, lanes))
    starts_col = jnp.sum(jnp.where(col_i < row_i, table, 0.0), axis=1, keepdims=True)
    len_col = jnp.sum(jnp.where(col_i == row_i, table, 0.0), axis=1, keepdims=True)
    starts_row = jnp.sum(jnp.where(row_i < col_i, len_col, 0.0), axis=0, keepdims=True)
    first = jnp.float32(1) * first_row
    pos_col = iota((tok, lanes), 0).astype(jnp.float32) + first
    pos_row = iota((lanes, tok), 1).astype(jnp.float32) + first
    roll_col = jnp.sum(jnp.where(starts_row <= pos_col, 1.0, 0.0), axis=1, keepdims=True) - 1.0
    roll_row = jnp.sum(jnp.where(starts_col <= pos_row, 1.0, 0.0), axis=0, keepdims=True) - 1.0
    return starts_row, roll_col, roll_row, pos_col


def local_mix_kernel(len_ref, x_ref, b_ref, c_ref, dt_ref, rate_ref, skip_ref, y_ref, run_ref, e_ref, dl_ref, xw_ref):
    models, inner, tok = x_ref.shape
    heads = dt_ref.shape[0]
    head = inner // heads
    state = b_ref.shape[1]
    first_row = lax.axis_index("seq") * tok
    _, roll_col, roll_row, _ = rollout_tables(len_ref[...].astype(jnp.float32), first_row, tok)
    s_i, t_i = iota((tok, tok), 0), iota((tok, tok), 1)
    mask = (roll_col == roll_row) & (s_i <= t_i)
    mask_f = mask.astype(jnp.float32)
    eye = (s_i == t_i).astype(jnp.float32)
    tail = roll_row == roll_row[:, tok - 1 : tok]
    lasts = []
    for m in range(models):
        dt = dt_ref[:, m, :]
        heads_eye = iota((heads, heads), 0) == iota((heads, heads), 1)
        rate = jnp.sum(jnp.where(heads_eye, rate_ref[m : m + 1, :], 0.0), axis=1, keepdims=True)
        run = jnp.dot(-dt * rate, mask_f, precision=HIGHEST, preferred_element_type=jnp.float32)
        up = jnp.log(dt) - run
        up_cols = lax.dot_general(
            eye, up, (((1,), (1,)), ((), ())), precision=HIGHEST, preferred_element_type=jnp.float32
        )
        gram = lax.dot_general(
            b_ref[m], c_ref[m], (((0,), (0,)), ((), ())), preferred_element_type=jnp.float32
        )
        last = run[:, tok - 1 : tok]
        end_w = jnp.where(tail, jnp.exp(jnp.where(tail, last + up, LOW)), 0.0)
        for h in range(heads):
            rows = slice(h * head, (h + 1) * head)
            gap = jnp.where(mask, run[h : h + 1, :] + up_cols[:, h : h + 1], LOW)
            weights = (jnp.exp(gap) * gram).astype(jnp.bfloat16)
            x_h = x_ref[m, rows, :]
            x_f = x_h.astype(jnp.float32)
            y_ref[m, rows, :] = (
                jnp.dot(x_h, weights, preferred_element_type=jnp.float32) + skip_ref[m, h] * x_f
            )
            xw_ref[rows, :] = (x_f * end_w[h : h + 1, :]).astype(jnp.bfloat16)
        e_ref[:, m * state : (m + 1) * state] = lax.dot_general(
            xw_ref[...], b_ref[m], (((1,), (1,)), ((), ())), preferred_element_type=jnp.float32
        ).astype(jnp.bfloat16)
        run_ref[m, 0:heads, :] = run
        lasts.append(last)
    dl_ref[...] = jnp.zeros(dl_ref.shape, jnp.float32)
    dl_ref[0:heads, :] = jnp.where(iota((heads, models * state), 1) < state, lasts[0], lasts[1])


def vmem():
    return pl.BlockSpec(memory_space=pltpu.VMEM)


def anywhere():
    return pl.BlockSpec(memory_space=pl.ANY)


def smem():
    return pl.BlockSpec(memory_space=pltpu.SMEM)


def local_mix(len_row, x, b, c, dt, rate, skip):
    models, inner, tok = x.shape
    state = b.shape[1]
    return pl.pallas_call(
        local_mix_kernel,
        out_shape=(
            jax.ShapeDtypeStruct((models, inner, tok), jnp.float32),
            jax.ShapeDtypeStruct((models, 8, tok), jnp.float32),
            jax.ShapeDtypeStruct((inner, models * state), jnp.bfloat16),
            jax.ShapeDtypeStruct((8, models * state), jnp.float32),
        ),
        in_specs=[vmem()] * 6 + [smem()],
        out_specs=(vmem(),) * 4,
        scratch_shapes=[pltpu.VMEM((inner, tok), jnp.bfloat16)],
        compiler_params=pltpu.CompilerParams(vmem_limit_bytes=VMEM_BYTES),
        cost_estimate=pl.CostEstimate(flops=2 * 10**9, bytes_accessed=4 * 10**6, transcendentals=10**6),
        name="local_mix",
    )(len_row, x, b, c, dt, rate, skip)


def greet(barrier, peers):
    for peer in peers:
        pl.semaphore_signal(barrier, inc=1, device_id=peer, device_id_type=MESH)
    pl.semaphore_wait(barrier, len(peers))


def make_sender(send_sem, recv_sem):
    taken, begun = [0], []

    def send(src, dst, peer):
        k = taken[0]
        taken[0] += 1
        copy = pltpu.make_async_remote_copy(
            src_ref=src, dst_ref=dst, send_sem=send_sem.at[k], recv_sem=recv_sem.at[k],
            device_id=peer, device_id_type=MESH,
        )
        copy.start()
        begun.append(copy)
        return copy

    return send, begun


RING_COPIES = 3 + 2 + 2 + 8 + 8 + 16 + 16


def place():
    seq, mp = lax.axis_index("seq"), lax.axis_index("mp")
    z, y = seq // Y, lax.rem(seq, Y)

    def at_y(d):
        return (z * Y + lax.rem(y + d + Y, Y), mp)

    def at_z(d):
        return (lax.rem(z + d + Z, Z) * Y + y, mp)

    return seq, mp, z, y, at_y, at_z


def torus_ring(send, own_ref, all_ref, split, own_sem):
    _, _, z, y, at_y, at_z = place()
    rows = own_ref.shape[0]
    half = (rows - split) // 2
    first, second = pl.ds(0, split), pl.ds(split, rows - split)
    low, high = pl.ds(split, half), pl.ds(split + half, rows - split - half)

    def zz(d):
        return lax.rem(z + d + Z, Z)

    def yy(d):
        return lax.rem(y + d + Y, Y)

    def along(ref, peer):
        return send(ref, ref, peer)

    pending, last = [], []

    def to_y(d):
        src = all_ref.at[zz(d), y, second] if d else own_ref.at[second]
        dst = all_ref.at[zz(d), y, second]
        pending.append((zz(d), send(src, dst, at_y(1)), send(src, dst, at_y(-1))))

    def pass_y():
        j, up, down = pending.pop(0)
        up.wait_recv()
        last.append(along(all_ref.at[j, yy(-1), low], at_y(1)))
        down.wait_recv()
        last.append(along(all_ref.at[j, yy(1), high], at_y(-1)))

    keep = pltpu.make_async_copy(own_ref, all_ref.at[z, y], own_sem)
    keep.start()
    firsts = [send(own_ref.at[first], all_ref.at[z, y, first], at_y(d)) for d in (1, -1, 2)]
    right = send(own_ref.at[second], all_ref.at[z, y, second], at_z(1))
    left = send(own_ref.at[second], all_ref.at[z, y, second], at_z(-1))
    to_y(0)
    keep.wait()
    yield
    for copy in firsts:
        copy.wait_recv()
    group = all_ref.at[z, :, first]
    far_right, far_left = along(group, at_z(1)), along(group, at_z(-1))
    yield
    for k in range(1, Z // 2):
        right.wait_recv()
        right = along(all_ref.at[zz(-k), y, second if k < Z // 2 - 1 else low], at_z(1))
        to_y(-k)
        left.wait_recv()
        left = along(all_ref.at[zz(k), y, second if k < Z // 2 - 1 else high], at_z(-1))
        to_y(k)
        yield
        pass_y()
        yield
        if k > 1:
            far_right.wait_recv()
            far_right = along(all_ref.at[zz(1 - k), :, first], at_z(1))
            far_left.wait_recv()
            far_left = along(all_ref.at[zz(k - 1), :, first], at_z(-1))
            yield
    right.wait_recv()
    left.wait_recv()
    to_y(Z // 2)
    yield
    pass_y()
    pass_y()
    yield
    far_right.wait_recv()
    far_right = along(all_ref.at[zz(1 - Z // 2), pl.ds(0, Y // 2), first], at_z(1))
    far_left.wait_recv()
    far_left = along(all_ref.at[zz(Z // 2 - 1), pl.ds(Y // 2, Y // 2), first], at_z(-1))
    yield
    while pending:
        pass_y()
        yield
    far_right.wait_recv()
    far_left.wait_recv()
    for copy in last:
        copy.wait_recv()


def states_kernel(
    pt_ref, e_ref, dl_ref, wo_ref, dw_ref,
    pall_ref, en_ref, dn_ref, wos_ref, dws_ref,
    send_sem, recv_sem, own_sem,
):
    seq, mp, _, _, at_y, at_z = place()
    count = Y * Z

    def at_s(d):
        return (lax.rem(seq + d + count, count), mp)

    sibling = (seq, mp + 1 - 2 * lax.rem(mp, CORES))
    greet(
        pltpu.get_barrier_semaphore(),
        [at_y(1), at_y(-1), at_y(2), at_z(1), at_z(-1), sibling]
        + [at_s(d) for d in range(1, REACH + 1)]
        + [at_s(-d) for d in range(1, REACH + 1)],
    )
    send, begun = make_sender(send_sem, recv_sem)
    ring = torus_ring(send, pt_ref, pall_ref, PROMPT_SPLIT, own_sem)
    next(ring)
    waits = []
    for d in range(1, REACH + 1):
        waits.append(send(e_ref, en_ref.at[d - 1], at_s(d)))
        waits.append(send(dl_ref, dn_ref.at[d - 1], at_s(d)))
    waits.append(send(wo_ref, wos_ref, sibling))
    waits.append(send(dw_ref, dws_ref, sibling))
    for _ in ring:
        pass
    for copy in waits:
        copy.wait_recv()
    for copy in begun:
        copy.wait_send()


PROMPT_SPLIT = 192
HEAD_SPLIT = 48
HEAD_NATIVE = 1024
TILE = 256


def states(pt, e, dl, wo, dw):
    out = (
        jax.ShapeDtypeStruct((Z, Y) + pt.shape, pt.dtype),
        jax.ShapeDtypeStruct((REACH,) + e.shape, e.dtype),
        jax.ShapeDtypeStruct((REACH,) + dl.shape, dl.dtype),
        jax.ShapeDtypeStruct(wo.shape, wo.dtype),
        jax.ShapeDtypeStruct(dw.shape, dw.dtype),
    )
    copies = RING_COPIES + 2 * REACH + 2
    return pl.pallas_call(
        states_kernel,
        out_shape=out,
        in_specs=[anywhere()] * 5,
        out_specs=(anywhere(),) * 5,
        scratch_shapes=[
            pltpu.SemaphoreType.DMA((copies,)),
            pltpu.SemaphoreType.DMA((copies,)),
            pltpu.SemaphoreType.DMA,
        ],
        compiler_params=pltpu.CompilerParams(
            collective_id=1, has_side_effects=True, vmem_limit_bytes=VMEM_BYTES
        ),
        cost_estimate=pl.CostEstimate(flops=0, bytes_accessed=10**8, transcendentals=0),
        name="state_exchange",
    )(pt, e, dl, wo, dw)


def finish_mix_kernel(
    len_s, hold_s, len_ref, y_ref, run_ref, c_ref, z_ref, pall_ref, en_ref, dn_ref, g_ref, acc_ref
):
    models, inner, tok = y_ref.shape
    lanes_all = pall_ref.shape[2]
    head = lanes_all // models
    heads = inner // head
    first_row = lax.axis_index("seq") * tok
    starts_row, _, roll_row, _ = rollout_tables(len_ref[...].astype(jnp.float32), first_row, tok)
    first = jnp.float32(1) * first_row
    start0 = jnp.max(jnp.where(starts_row <= first, starts_row, -1.0), axis=1, keepdims=True)
    inherits = start0 < first
    roll0 = jnp.where(inherits, roll_row[:, 0:1], -1.0)
    inherited = roll_row == roll0

    def scan(r, carry):
        start, lo, hi, hold0 = carry
        lo = jnp.where(start < first_row, r + 1, lo)
        hi = jnp.where(start < first_row + tok, r + 1, hi)
        hold0 = jnp.where(start < first_row, hold_s[0, r], hold0)
        return start + len_s[0, r], lo, hi, hold0

    rolls = len_s.shape[1]
    _, lo, hi, hold0 = lax.fori_loop(
        0, rolls, scan, (jnp.int32(0), jnp.int32(0), jnp.int32(0), jnp.int32(-1))
    )
    hold0 = jnp.where(hold0 < 0, -1, hold0)
    source = jnp.maximum(hold0, 0)
    arriving = []
    for h in range(heads):
        rows = slice(h * head, (h + 1) * head)
        total = jnp.zeros((1, lanes_all), jnp.float32)
        part = jnp.zeros((head, lanes_all), jnp.float32)
        for k in range(1, REACH + 1):
            near = start0 < first - jnp.float32((k - 1) * tok)
            part = part + jnp.where(near, jnp.exp(total) * en_ref[k - 1, rows, :].astype(jnp.float32), 0.0)
            total = jnp.where(near, total + dn_ref[k - 1, h : h + 1, :], total)
        begun = jnp.exp(total) * pall_ref[source, rows, :].astype(jnp.float32)
        arriving.append(part + jnp.where(inherits & (hold0 >= 0), begun, 0.0))
    arriving = jnp.concatenate(arriving, axis=0)
    high = arriving.astype(jnp.bfloat16)
    low = (arriving - high.astype(jnp.float32)).astype(jnp.bfloat16)
    c_all = jnp.concatenate([c_ref[m].astype(jnp.float32) for m in range(models)], axis=0)
    of_model = iota((lanes_all, tok), 0) // c_ref.shape[1]

    def masked(tokens, m):
        return jnp.where(tokens & (of_model == m), c_all, 0.0).astype(jnp.bfloat16)

    for m in range(models):
        c_in = masked(inherited, m)
        acc_ref[m] = jnp.dot(high, c_in, preferred_element_type=jnp.float32) + jnp.dot(
            low, c_in, preferred_element_type=jnp.float32
        )

    def borrow(r, carry):
        held = hold_s[0, r]

        @pl.when(held >= 0)
        def _():
            mine = roll_row == r.astype(jnp.float32)
            for m in range(models):
                acc_ref[m] += jnp.dot(pall_ref[held], masked(mine, m), preferred_element_type=jnp.float32)

        return carry

    lax.fori_loop(lo, hi, borrow, 0)
    for m in range(models):
        for h in range(heads):
            rows = slice(h * head, (h + 1) * head)
            gate = z_ref[m, rows, :].astype(jnp.float32)
            out = y_ref[m, rows, :] + jnp.exp(run_ref[m, h : h + 1, :]) * acc_ref[m, rows, :]
            acc_ref[m, rows, :] = out * (gate / (1.0 + jnp.exp(-gate)))
        g_ref[m] = jnp.transpose(acc_ref[m]).astype(jnp.bfloat16)


def finish_mix(len_row, lengths, holders, y, run, c, z, pall, en, dn):
    models, inner, tok = y.shape
    return pl.pallas_call(
        finish_mix_kernel,
        out_shape=jax.ShapeDtypeStruct((models, tok, inner), jnp.bfloat16),
        in_specs=[smem()] * 2 + [vmem()] * 8,
        out_specs=vmem(),
        scratch_shapes=[pltpu.VMEM((models, inner, tok), jnp.float32)],
        compiler_params=pltpu.CompilerParams(vmem_limit_bytes=VMEM_BYTES),
        cost_estimate=pl.CostEstimate(flops=10**9, bytes_accessed=8 * 10**6, transcendentals=10**6),
        name="finish_mix",
    )(lengths, holders, len_row, y, run, c, z, pall, en, dn)


def project_kernel(
    g_ref, wo_ref, wos_ref, dw_ref, dws_ref, up_ref, res_ref, scale_ref, head_ref, nall_ref, wall_ref,
    gs_ref, low_ref, acc_ref, out_ref, comb_ref, relay_ref, direct_ref, sum_ref, h_ref, n_ref,
    send_sem, recv_sem, ring_send, ring_recv, own_sem, keep_sem,
):
    seq, mp, _, _, at_y, at_z = place()
    x, core = mp // CORES, lax.rem(mp, CORES)
    chunks = acc_ref.shape[0]
    width = acc_ref.shape[4]
    share = res_ref.shape[1]
    model_width = res_ref.shape[2]
    inner = g_ref.shape[4]
    rows = X * share
    sibling = (seq, x * CORES + 1 - core)

    def xx(d):
        return lax.rem(x + d + X, X)

    def at_x(d):
        return (seq, xx(d) * CORES + core)

    greet(
        pltpu.get_barrier_semaphore(),
        [sibling, at_x(1), at_x(-1), at_y(1), at_y(-1), at_y(2), at_z(1), at_z(-1)],
    )
    send, begun = make_sender(send_sem, recv_sem)
    ring_out, ring_begun = make_sender(ring_send, ring_recv)
    gated = send(g_ref.at[:, :, 1 - core], gs_ref, sibling)
    ring = torus_ring(ring_out, head_ref, wall_ref, HEAD_SPLIT, own_sem)

    def ring_step(times=1):
        for _ in range(times):
            next(ring, None)

    ring_step()
    own_g = g_ref[:, :, core].reshape(2 * rows, inner)
    low = jnp.dot(own_g[:rows], dw_ref[...], preferred_element_type=jnp.float32)
    gated.wait_recv()
    sib_g = gs_ref[...].reshape(2 * rows, inner)
    low = low + jnp.dot(sib_g[:rows], dws_ref[...], preferred_element_type=jnp.float32)
    low_ref[...] = low.astype(jnp.bfloat16)

    relays, directs, sums = [], [], []

    def combine(n):
        for side, d, m in ((0, 1, 0), (1, -1, 1)):
            relays[n][side].wait_recv()
            total = acc_ref[n, m, xx(d)] + relay_ref[n, side].astype(jnp.float32)
            comb_ref[n, side] = total.astype(jnp.bfloat16)
        sums.append(
            [send(comb_ref.at[n, side], sum_ref.at[n, side], at_x(d)) for side, d in ((0, 1), (1, -1))]
        )

    for n in range(chunks):
        cols = slice(n * width, (n + 1) * width)
        acc = jnp.dot(
            g_ref[:, :, core].reshape(2 * rows, inner), wo_ref[:, cols], preferred_element_type=jnp.float32
        ) + jnp.dot(gs_ref[...].reshape(2 * rows, inner), wos_ref[:, cols], preferred_element_type=jnp.float32)
        more = jnp.dot(low_ref[...], up_ref[:, cols], preferred_element_type=jnp.float32)
        acc_ref[n, 0] = (acc[:rows] + more).reshape(X, share, width)
        acc_ref[n, 1] = acc[rows:].reshape(X, share, width)
        out_ref[n] = acc_ref[n].astype(jnp.bfloat16)
        far = xx(2)
        relays.append(
            [send(out_ref.at[n, m, far], relay_ref.at[n, side], at_x(d)) for side, d, m in ((0, 1, 0), (1, -1, 1))]
        )
        directs.append(
            [
                send(out_ref.at[n, m, xx(d)], direct_ref.at[n, side], at_x(d))
                for side, d, m in ((0, 1, 1), (1, -1, 0))
            ]
        )
        if n >= 1:
            combine(n - 1)
        if n in (1, 3, 5):
            ring_step()
    combine(chunks - 1)
    ring_step()

    square = jnp.zeros((2, share, 1), jnp.float32)
    for n in range(chunks):
        cols = slice(n * width, (n + 1) * width)
        for copy in sums[n] + directs[n]:
            copy.wait_recv()
        squares = []
        for m in range(2):
            total = (
                acc_ref[n, m, x]
                + sum_ref[n, m].astype(jnp.float32)
                + direct_ref[n, 1 - m].astype(jnp.float32)
                + res_ref[m, :, cols].astype(jnp.float32)
            )
            h_ref[m, :, cols] = total
            squares.append(jnp.sum(total * total, axis=1, keepdims=True))
        square = square + jnp.stack(squares)
        if n in (1, 3, 5):
            ring_step()
    n_ref[...] = (h_ref[...] * lax.rsqrt(square / model_width + 1e-05) * scale_ref[...]).astype(jnp.bfloat16)

    def block(d, m):
        return nall_ref.at[m, xx(d) * CORES + core]

    near = [[None, None], [None, None]]
    for side, d, m in ((0, 1, 0), (1, -1, 1), (0, 1, 1), (1, -1, 0)):
        near[side][m] = send(n_ref.at[m], block(0, m), at_x(d))
    shared = [send(n_ref.at[m], block(0, m), sibling) for m in range(2)]
    keep = pltpu.make_async_copy(n_ref, nall_ref.at[:, mp], keep_sem)
    keep.start()
    ring_step()
    far = []
    for side, d, m in ((0, 1, 0), (1, -1, 1)):
        near[side][m].wait_recv()
        far.append(send(block(-d, m), block(-d, m), at_x(d)))
        shared.append(send(block(-d, m), block(-d, m), sibling))
    ring_step(2)
    for side, d, m in ((0, 1, 1), (1, -1, 0)):
        near[side][m].wait_recv()
        shared.append(send(block(-d, m), block(-d, m), sibling))
    ring_step(2)
    for side, m in ((0, 0), (1, 1)):
        far[side].wait_recv()
        shared.append(send(block(2, m), block(2, m), sibling))
    for _ in ring:
        pass
    keep.wait()
    for copy in shared:
        copy.wait_recv()
    for copy in begun + ring_begun:
        copy.wait_send()


def project(gated, wo, wos, dw, dws, up, res, scale, head):
    models, tok, inner = gated.shape
    width_all = wo.shape[1]
    share = res.shape[1]
    width = 512
    chunks = width_all // width
    bf16, f32 = jnp.bfloat16, jnp.float32
    dma = pltpu.SemaphoreType.DMA
    copies = 1 + 6 * chunks + 4 + 2 + 2 + 6
    piece = pltpu.VMEM((chunks, 2, share, width), bf16)
    return pl.pallas_call(
        project_kernel,
        out_shape=(
            jax.ShapeDtypeStruct((models, X * CORES, share, width_all), bf16),
            jax.ShapeDtypeStruct((Z, Y) + head.shape, bf16),
        ),
        in_specs=[vmem()] * 8 + [anywhere()],
        out_specs=(anywhere(),) * 2,
        scratch_shapes=[
            pltpu.VMEM((models, X, share, inner), bf16),
            pltpu.VMEM((X * share, dw.shape[1]), bf16),
            pltpu.VMEM((chunks, models, X, share, width), f32),
            pltpu.VMEM((chunks, models, X, share, width), bf16),
            piece, piece, piece, piece,
            pltpu.VMEM((models, share, width_all), f32),
            pltpu.VMEM((models, share, width_all), bf16),
            dma((copies,)), dma((copies,)), dma((RING_COPIES,)), dma((RING_COPIES,)), dma, dma,
        ],
        compiler_params=pltpu.CompilerParams(
            collective_id=2, has_side_effects=True, vmem_limit_bytes=VMEM_BYTES
        ),
        cost_estimate=pl.CostEstimate(flops=10**10, bytes_accessed=10**8, transcendentals=0),
        name="project_norm",
    )(gated.reshape(models, X, CORES, share, inner), wo, wos, dw, dws, up, res, scale, head)


def scores_kernel(
    vocab, native, n_ref, w1_ref, w2_ref, tgt_ref, valid_ref, len_ref, owner_ref, sums_ref, delta_ref,
    max_ref, sum_ref, hit_ref, stat_ref, all_ref, part_ref, parts_ref, s_send, s_recv, p_send, p_recv,
):
    seq, mp = lax.axis_index("seq"), lax.axis_index("mp")
    peers, count = X * CORES, Y * Z
    step = pl.program_id(0)
    tile = w1_ref.shape[1]
    rows = n_ref.shape[0]
    barrier = pltpu.get_barrier_semaphore()

    @pl.when(step == 0)
    def _():
        for d in range(1, peers):
            pl.semaphore_signal(barrier, inc=1, device_id=(seq, lax.rem(mp + d, peers)), device_id_type=MESH)

        def hello(d, carry):
            pl.semaphore_signal(barrier, inc=1, device_id=(lax.rem(seq + d, count), mp), device_id_type=MESH)
            return carry

        lax.fori_loop(1, count, hello, 0)
        max_ref[...] = jnp.full(max_ref.shape, -3e38, jnp.float32)
        sum_ref[...] = jnp.zeros(sum_ref.shape, jnp.float32)
        hit_ref[...] = jnp.zeros(hit_ref.shape, jnp.float32)

    def add(w_ref):
        logits = jnp.dot(n_ref[...], w_ref[...], preferred_element_type=jnp.float32)
        col = iota((rows, tile), 1) + step * tile
        real = col < vocab
        logits = jnp.where(real, logits, -3e38)
        top = jnp.maximum(max_ref[...], jnp.max(logits, axis=1, keepdims=True))
        sum_ref[...] = sum_ref[...] * jnp.exp(max_ref[...] - top) + jnp.sum(
            jnp.where(real, jnp.exp(logits - top), 0.0), axis=1, keepdims=True
        )
        max_ref[...] = top
        hit_ref[...] += jnp.sum(jnp.where(real & (col == tgt_ref[...]), logits, 0.0), axis=1, keepdims=True)

    @pl.when(step < native)
    def _():
        add(w1_ref)

    @pl.when(step >= native)
    def _():
        add(w2_ref)

    @pl.when(step == pl.num_programs(0) - 1)
    def _():
        lane = iota((rows, 128), 1)
        packed = jnp.where(
            lane == 0, max_ref[...], jnp.where(lane == 1, sum_ref[...], jnp.where(lane == 2, hit_ref[...], 0.0))
        )
        stat_ref[...] = jnp.transpose(packed)[0:8]
        pl.semaphore_wait(barrier, peers - 1 + count - 1)
        combine_scores(
            stat_ref, valid_ref, len_ref, owner_ref, sums_ref, delta_ref,
            all_ref, part_ref, parts_ref, s_send, s_recv, p_send, p_recv,
        )


def combine_scores(
    stat_ref, valid_ref, len_ref, owner_ref, sums_ref, delta_ref,
    all_ref, part_ref, parts_ref, s_send, s_recv, p_send, p_recv,
):
    seq, mp = lax.axis_index("seq"), lax.axis_index("mp")
    peers, count = X * CORES, Y * Z
    tok = valid_ref.shape[1]

    def stats(d):
        return pltpu.make_async_remote_copy(
            src_ref=stat_ref, dst_ref=all_ref.at[mp], send_sem=s_send.at[d], recv_sem=s_recv.at[d],
            device_id=(seq, lax.rem(mp + d, peers)), device_id_type=MESH,
        )

    for d in range(1, peers):
        stats(d).start()
    all_ref[mp] = stat_ref[...]
    starts_row, roll_col, _, _ = rollout_tables(len_ref[...].astype(jnp.float32), seq * tok, tok)
    lanes = starts_row.shape[1]
    member = (roll_col == iota((tok, lanes), 1).astype(jnp.float32)).astype(jnp.float32)
    for d in range(1, peers):
        stats(d).wait_recv()
    tops = [all_ref[k][0:1] for k in range(peers)]
    top = functools.reduce(jnp.maximum, tops)
    total = functools.reduce(
        jnp.add, [all_ref[k][1:2] * jnp.exp(tops[k] - top) for k in range(peers)]
    )
    hit = functools.reduce(jnp.add, [all_ref[k][2:3] for k in range(peers)])
    logprob = hit - top - jnp.log(total)
    delta = (logprob[:, :tok] - logprob[:, tok:]) * valid_ref[...].astype(jnp.float32)
    delta_ref[...] = delta
    part_ref[...] = jnp.dot(
        jnp.broadcast_to(delta, (8, tok)), member, precision=HIGHEST, preferred_element_type=jnp.float32
    )

    def parts(d):
        return pltpu.make_async_remote_copy(
            src_ref=part_ref, dst_ref=parts_ref.at[seq], send_sem=p_send.at[d], recv_sem=p_recv.at[d],
            device_id=(lax.rem(seq + d, count), mp), device_id_type=MESH,
        )

    def begin(d, carry):
        parts(d).start()
        return carry

    def end(d, carry):
        parts(d).wait_recv()
        return carry

    def drain(d, carry):
        parts(d).wait_send()
        return carry

    lax.fori_loop(1, count, begin, 0)
    parts_ref[seq] = part_ref[...]
    lax.fori_loop(1, count, end, 0)
    sums = functools.reduce(jnp.add, [parts_ref[k] for k in range(count)])[0:1] / len_ref[...].astype(jnp.float32)
    mine = jnp.where(owner_ref[...] == seq, sums, 0.0)
    sums_ref[...] = mine[:, : sums_ref.shape[1]]
    for d in range(1, peers):
        stats(d).wait_send()
    lax.fori_loop(1, count, drain, 0)


def scores(normed, w1, w2, vocab, target, valid_row, len_row, owner_row, rolls):
    peers, count = X * CORES, Y * Z
    rows, depth = normed.shape
    tok = valid_row.shape[1]
    lanes = len_row.shape[1]
    native = w1.shape[1] // TILE
    dma = pltpu.SemaphoreType.DMA
    f32 = jnp.float32

    def fixed(shape):
        return pl.BlockSpec(shape, lambda j: (0, 0), pipeline_mode=pl.Buffered(1))

    return pl.pallas_call(
        functools.partial(scores_kernel, vocab, native),
        grid=(native + w2.shape[1] // TILE,),
        out_shape=(jax.ShapeDtypeStruct((1, rolls), f32), jax.ShapeDtypeStruct((1, tok), f32)),
        in_specs=[
            fixed((rows, depth)),
            pl.BlockSpec((depth, TILE), lambda j: (0, jnp.minimum(j, native - 1))),
            pl.BlockSpec((depth, TILE), lambda j: (0, jnp.maximum(j - native, 0))),
            fixed((rows, 1)), fixed((1, tok)), fixed((1, lanes)), fixed((1, lanes)),
        ],
        out_specs=(pl.BlockSpec((1, rolls), lambda j: (0, 0)), pl.BlockSpec((1, tok), lambda j: (0, 0))),
        scratch_shapes=[pltpu.VMEM((rows, 1), f32)] * 3
        + [
            pltpu.VMEM((8, rows), f32),
            pltpu.VMEM((peers, 8, rows), f32),
            pltpu.VMEM((8, lanes), f32),
            pltpu.VMEM((count, 8, lanes), f32),
            dma((peers,)), dma((peers,)), dma((count,)), dma((count,)),
        ],
        compiler_params=pltpu.CompilerParams(
            collective_id=3, has_side_effects=True, vmem_limit_bytes=VMEM_BYTES
        ),
        cost_estimate=pl.CostEstimate(flops=8 * 10**9, bytes_accessed=2 * 10**7, transcendentals=10**6),
        name="scores",
    )(normed, w1, w2, target, valid_row, len_row, owner_row)


def shards(
    scored_token_targets, valid, lengths, owners, holders, mixer_input_x, mixer_gate_input,
    input_projection_b, output_projection_c, token_step_sizes, head_decay_rate, head_skip_scale,
    prompt_held_states, shared_output_weight, adapter_down_weight, adapter_up_weight,
    residual, final_norm_scale, vocab_head_weight,
):
    tok = scored_token_targets.shape[0]
    models, _, inner = mixer_input_x.shape
    state = input_projection_b.shape[2]
    rolls = lengths.shape[0]
    share = tok // (X * CORES)
    mp = lax.axis_index("mp")
    vocab = vocab_head_weight.shape[1]
    head_native = lax.all_gather(vocab_head_weight[:, :HEAD_NATIVE], "seq", axis=0, tiled=True)
    rest = vocab - HEAD_NATIVE
    head_rest = jnp.pad(vocab_head_weight[:, HEAD_NATIVE:], ((0, 0), (0, -rest % TILE)))

    def row(values, fill):
        return jnp.pad(values, (0, 128 - rolls), constant_values=fill)[None, :]

    len_row, owner_row = row(lengths, 0), row(owners, -1)
    prompts = jnp.transpose(prompt_held_states[:, 0], (1, 2, 0, 3)).reshape(inner, models * state)
    own_res = jnp.transpose(lax.dynamic_slice_in_dim(residual, mp * share, share, 0), (1, 0, 2))
    x, b, c, z = (
        jnp.swapaxes(a, 1, 2)
        for a in (mixer_input_x, input_projection_b, output_projection_c, mixer_gate_input)
    )
    y, run, ends, last = local_mix(
        len_row, x, b, c, jnp.transpose(token_step_sizes, (2, 0, 1)), head_decay_rate, head_skip_scale
    )
    pall, en, dn, wos, dws = states(prompts, ends, last, shared_output_weight, adapter_down_weight)
    gated = finish_mix(
        len_row, lengths[None, :], holders[None, :], y, run, c, z,
        pall.reshape((Z * Y,) + prompts.shape), en, dn,
    )
    normed, head_own = project(
        gated, shared_output_weight, wos, adapter_down_weight, dws, adapter_up_weight, own_res,
        final_norm_scale[None, :], head_rest,
    )
    local = scored_token_targets - mp * vocab
    target = jnp.concatenate([local, local])[:, None]
    sums, delta = scores(
        normed.reshape(models * tok, -1), head_native, head_own.reshape(-1, head_rest.shape[1]), vocab,
        target, valid[None, :], len_row, owner_row, rolls,
    )
    return sums, delta.reshape(tok)


def solution(mesh):
    placed = (
        P("seq"), P("seq"), P(), P(), P(),
        P(None, "seq", "mp"), P(None, "seq", "mp"),
        P(None, "seq", None), P(None, "seq", None), P(None, "seq", "mp"),
        P(None, "mp"), P(None, "mp"), P(None, "seq", "mp", None, None),
        P("mp", None), P("mp", None), P(), P("seq", None, None), P(), P("seq", "mp"),
    )
    return jax.shard_map(
        shards, mesh=mesh, in_specs=placed, out_specs=(P("seq", None), P("seq")), check_vma=False
    )
```

```python
import functools

import jax
import jax.numpy as jnp
from jax import lax
from jax.experimental import pallas as pl
from jax.experimental.pallas import tpu as pltpu
from jax.sharding import PartitionSpec as P

HIGHEST = lax.Precision.HIGHEST
MESH = pl.DeviceIdType.MESH
Y, Z = 4, 8
X, CORES = 4, 2
REACH = 4
VMEM_BYTES = 56 * 1024 * 1024
LOW = -1e30


def iota(shape, dim):
    return lax.broadcasted_iota(jnp.int32, shape, dim)


def rollout_tables(len_row, first_row, tok):
    lanes = len_row.shape[1]
    row_i, col_i = iota((lanes, lanes), 0), iota((lanes, lanes), 1)
    table = jnp.broadcast_to(len_row, (lanes, lanes))
    starts_col = jnp.sum(jnp.where(col_i < row_i, table, 0.0), axis=1, keepdims=True)
    len_col = jnp.sum(jnp.where(col_i == row_i, table, 0.0), axis=1, keepdims=True)
    starts_row = jnp.sum(jnp.where(row_i < col_i, len_col, 0.0), axis=0, keepdims=True)
    first = jnp.float32(1) * first_row
    pos_col = iota((tok, lanes), 0).astype(jnp.float32) + first
    pos_row = iota((lanes, tok), 1).astype(jnp.float32) + first
    roll_col = jnp.sum(jnp.where(starts_row <= pos_col, 1.0, 0.0), axis=1, keepdims=True) - 1.0
    roll_row = jnp.sum(jnp.where(starts_col <= pos_row, 1.0, 0.0), axis=0, keepdims=True) - 1.0
    return starts_row, roll_col, roll_row, pos_col


def local_mix_kernel(len_ref, x_ref, b_ref, c_ref, dt_ref, rate_ref, skip_ref, y_ref, run_ref, e_ref, dl_ref, xw_ref):
    models, inner, tok = x_ref.shape
    heads = dt_ref.shape[0]
    head = inner // heads
    state = b_ref.shape[1]
    first_row = lax.axis_index("seq") * tok
    _, roll_col, roll_row, _ = rollout_tables(len_ref[...].astype(jnp.float32), first_row, tok)
    s_i, t_i = iota((tok, tok), 0), iota((tok, tok), 1)
    mask = (roll_col == roll_row) & (s_i <= t_i)
    mask_f = mask.astype(jnp.float32)
    eye = (s_i == t_i).astype(jnp.float32)
    tail = roll_row == roll_row[:, tok - 1 : tok]
    lasts = []
    for m in range(models):
        dt = dt_ref[:, m, :]
        heads_eye = iota((heads, heads), 0) == iota((heads, heads), 1)
        rate = jnp.sum(jnp.where(heads_eye, rate_ref[m : m + 1, :], 0.0), axis=1, keepdims=True)
        run = jnp.dot(-dt * rate, mask_f, precision=HIGHEST, preferred_element_type=jnp.float32)
        up = jnp.log(dt) - run
        up_cols = lax.dot_general(
            eye, up, (((1,), (1,)), ((), ())), precision=HIGHEST, preferred_element_type=jnp.float32
        )
        gram = lax.dot_general(
            b_ref[m], c_ref[m], (((0,), (0,)), ((), ())), preferred_element_type=jnp.float32
        )
        last = run[:, tok - 1 : tok]
        end_w = jnp.where(tail, jnp.exp(jnp.where(tail, last + up, LOW)), 0.0)
        for h in range(heads):
            rows = slice(h * head, (h + 1) * head)
            gap = jnp.where(mask, run[h : h + 1, :] + up_cols[:, h : h + 1], LOW)
            weights = (jnp.exp(gap) * gram).astype(jnp.bfloat16)
            x_h = x_ref[m, rows, :]
            x_f = x_h.astype(jnp.float32)
            y_ref[m, rows, :] = (
                jnp.dot(x_h, weights, preferred_element_type=jnp.float32) + skip_ref[m, h] * x_f
            )
            xw_ref[rows, :] = (x_f * end_w[h : h + 1, :]).astype(jnp.bfloat16)
        e_ref[:, m * state : (m + 1) * state] = lax.dot_general(
            xw_ref[...], b_ref[m], (((1,), (1,)), ((), ())), preferred_element_type=jnp.float32
        ).astype(jnp.bfloat16)
        run_ref[m, 0:heads, :] = run
        lasts.append(last)
    dl_ref[...] = jnp.zeros(dl_ref.shape, jnp.float32)
    dl_ref[0:heads, :] = jnp.where(iota((heads, models * state), 1) < state, lasts[0], lasts[1])


def vmem():
    return pl.BlockSpec(memory_space=pltpu.VMEM)


def anywhere():
    return pl.BlockSpec(memory_space=pl.ANY)


def smem():
    return pl.BlockSpec(memory_space=pltpu.SMEM)


def local_mix(len_row, x, b, c, dt, rate, skip):
    models, inner, tok = x.shape
    state = b.shape[1]
    return pl.pallas_call(
        local_mix_kernel,
        out_shape=(
            jax.ShapeDtypeStruct((models, inner, tok), jnp.float32),
            jax.ShapeDtypeStruct((models, 8, tok), jnp.float32),
            jax.ShapeDtypeStruct((inner, models * state), jnp.bfloat16),
            jax.ShapeDtypeStruct((8, models * state), jnp.float32),
        ),
        in_specs=[vmem()] * 6 + [smem()],
        out_specs=(vmem(),) * 4,
        scratch_shapes=[pltpu.VMEM((inner, tok), jnp.bfloat16)],
        compiler_params=pltpu.CompilerParams(vmem_limit_bytes=VMEM_BYTES),
        cost_estimate=pl.CostEstimate(flops=2 * 10**9, bytes_accessed=4 * 10**6, transcendentals=10**6),
        name="local_mix",
    )(len_row, x, b, c, dt, rate, skip)


def greet(barrier, peers):
    for peer in peers:
        pl.semaphore_signal(barrier, inc=1, device_id=peer, device_id_type=MESH)
    pl.semaphore_wait(barrier, len(peers))


def make_sender(send_sem, recv_sem):
    taken, begun = [0], []

    def send(src, dst, peer):
        k = taken[0]
        taken[0] += 1
        copy = pltpu.make_async_remote_copy(
            src_ref=src, dst_ref=dst, send_sem=send_sem.at[k], recv_sem=recv_sem.at[k],
            device_id=peer, device_id_type=MESH,
        )
        copy.start()
        begun.append(copy)
        return copy

    return send, begun


RING_COPIES = 3 + 2 + 2 + 8 + 8 + 16 + 16


def place():
    seq, mp = lax.axis_index("seq"), lax.axis_index("mp")
    z, y = seq // Y, lax.rem(seq, Y)

    def at_y(d):
        return (z * Y + lax.rem(y + d + Y, Y), mp)

    def at_z(d):
        return (lax.rem(z + d + Z, Z) * Y + y, mp)

    return seq, mp, z, y, at_y, at_z


def torus_ring(send, own_ref, all_ref, split, own_sem):
    _, _, z, y, at_y, at_z = place()
    rows = own_ref.shape[0]
    half = (rows - split) // 2
    first, second = pl.ds(0, split), pl.ds(split, rows - split)
    low, high = pl.ds(split, half), pl.ds(split + half, rows - split - half)

    def zz(d):
        return lax.rem(z + d + Z, Z)

    def yy(d):
        return lax.rem(y + d + Y, Y)

    def along(ref, peer):
        return send(ref, ref, peer)

    pending, last = [], []

    def to_y(d):
        src = all_ref.at[zz(d), y, second] if d else own_ref.at[second]
        dst = all_ref.at[zz(d), y, second]
        pending.append((zz(d), send(src, dst, at_y(1)), send(src, dst, at_y(-1))))

    def pass_y():
        j, up, down = pending.pop(0)
        up.wait_recv()
        last.append(along(all_ref.at[j, yy(-1), low], at_y(1)))
        down.wait_recv()
        last.append(along(all_ref.at[j, yy(1), high], at_y(-1)))

    keep = pltpu.make_async_copy(own_ref, all_ref.at[z, y], own_sem)
    keep.start()
    firsts = [send(own_ref.at[first], all_ref.at[z, y, first], at_y(d)) for d in (1, -1, 2)]
    right = send(own_ref.at[second], all_ref.at[z, y, second], at_z(1))
    left = send(own_ref.at[second], all_ref.at[z, y, second], at_z(-1))
    to_y(0)
    keep.wait()
    yield
    for copy in firsts:
        copy.wait_recv()
    group = all_ref.at[z, :, first]
    far_right, far_left = along(group, at_z(1)), along(group, at_z(-1))
    yield
    for k in range(1, Z // 2):
        right.wait_recv()
        right = along(all_ref.at[zz(-k), y, second if k < Z // 2 - 1 else low], at_z(1))
        to_y(-k)
        left.wait_recv()
        left = along(all_ref.at[zz(k), y, second if k < Z // 2 - 1 else high], at_z(-1))
        to_y(k)
        yield
        pass_y()
        yield
        if k > 1:
            far_right.wait_recv()
            far_right = along(all_ref.at[zz(1 - k), :, first], at_z(1))
            far_left.wait_recv()
            far_left = along(all_ref.at[zz(k - 1), :, first], at_z(-1))
            yield
    right.wait_recv()
    left.wait_recv()
    to_y(Z // 2)
    yield
    pass_y()
    pass_y()
    yield
    far_right.wait_recv()
    far_right = along(all_ref.at[zz(1 - Z // 2), pl.ds(0, Y // 2), first], at_z(1))
    far_left.wait_recv()
    far_left = along(all_ref.at[zz(Z // 2 - 1), pl.ds(Y // 2, Y // 2), first], at_z(-1))
    yield
    while pending:
        pass_y()
        yield
    far_right.wait_recv()
    far_left.wait_recv()
    for copy in last:
        copy.wait_recv()


def states_kernel(
    pt_ref, e_ref, dl_ref, wo_ref, dw_ref, tgt_ref,
    pall_ref, en_ref, dn_ref, wos_ref, dws_ref, tgp_ref,
    send_sem, recv_sem, own_sem,
):
    seq, mp, _, y, at_y, at_z = place()
    count = Y * Z

    def at_s(d):
        return (lax.rem(seq + d + count, count), mp)

    sibling = (seq, mp + 1 - 2 * lax.rem(mp, CORES))
    greet(
        pltpu.get_barrier_semaphore(),
        [at_y(1), at_y(-1), at_y(2), at_z(1), at_z(-1), sibling]
        + [at_s(d) for d in range(1, REACH + 1)]
        + [at_s(-d) for d in range(1, REACH + 1)],
    )
    send, begun = make_sender(send_sem, recv_sem)
    ring = torus_ring(send, pt_ref, pall_ref, PROMPT_SPLIT, own_sem)
    next(ring)
    waits = []
    for d in range(1, REACH + 1):
        waits.append(send(e_ref, en_ref.at[d - 1], at_s(d)))
        waits.append(send(dl_ref, dn_ref.at[d - 1], at_s(d)))
    waits.append(send(wo_ref, wos_ref, sibling))
    waits.append(send(dw_ref, dws_ref, sibling))
    waits.append(send(tgt_ref, tgp_ref, partner_of(at_y, y)))
    for _ in ring:
        pass
    for copy in waits:
        copy.wait_recv()
    for copy in begun:
        copy.wait_send()


PROMPT_SPLIT = 192
PAIR_SPLIT = 64
TILE = 256


def states(pt, e, dl, wo, dw, tgt):
    out = (
        jax.ShapeDtypeStruct((Z, Y) + pt.shape, pt.dtype),
        jax.ShapeDtypeStruct((REACH,) + e.shape, e.dtype),
        jax.ShapeDtypeStruct((REACH,) + dl.shape, dl.dtype),
        jax.ShapeDtypeStruct(wo.shape, wo.dtype),
        jax.ShapeDtypeStruct(dw.shape, dw.dtype),
        jax.ShapeDtypeStruct(tgt.shape, tgt.dtype),
    )
    copies = RING_COPIES + 2 * REACH + 3
    return pl.pallas_call(
        states_kernel,
        out_shape=out,
        in_specs=[anywhere()] * 6,
        out_specs=(anywhere(),) * 6,
        scratch_shapes=[
            pltpu.SemaphoreType.DMA((copies,)),
            pltpu.SemaphoreType.DMA((copies,)),
            pltpu.SemaphoreType.DMA,
        ],
        compiler_params=pltpu.CompilerParams(
            collective_id=1, has_side_effects=True, vmem_limit_bytes=VMEM_BYTES
        ),
        cost_estimate=pl.CostEstimate(flops=0, bytes_accessed=10**8, transcendentals=0),
        name="state_exchange",
    )(pt, e, dl, wo, dw, tgt)


def finish_mix_kernel(
    len_s, hold_s, len_ref, y_ref, run_ref, c_ref, z_ref, pall_ref, en_ref, dn_ref, g_ref, acc_ref
):
    models, inner, tok = y_ref.shape
    lanes_all = pall_ref.shape[2]
    head = lanes_all // models
    heads = inner // head
    first_row = lax.axis_index("seq") * tok
    starts_row, _, roll_row, _ = rollout_tables(len_ref[...].astype(jnp.float32), first_row, tok)
    first = jnp.float32(1) * first_row
    start0 = jnp.max(jnp.where(starts_row <= first, starts_row, -1.0), axis=1, keepdims=True)
    inherits = start0 < first
    roll0 = jnp.where(inherits, roll_row[:, 0:1], -1.0)
    inherited = roll_row == roll0

    def scan(r, carry):
        start, lo, hi, hold0 = carry
        lo = jnp.where(start < first_row, r + 1, lo)
        hi = jnp.where(start < first_row + tok, r + 1, hi)
        hold0 = jnp.where(start < first_row, hold_s[0, r], hold0)
        return start + len_s[0, r], lo, hi, hold0

    rolls = len_s.shape[1]
    _, lo, hi, hold0 = lax.fori_loop(
        0, rolls, scan, (jnp.int32(0), jnp.int32(0), jnp.int32(0), jnp.int32(-1))
    )
    hold0 = jnp.where(hold0 < 0, -1, hold0)
    source = jnp.maximum(hold0, 0)
    arriving = []
    for h in range(heads):
        rows = slice(h * head, (h + 1) * head)
        total = jnp.zeros((1, lanes_all), jnp.float32)
        part = jnp.zeros((head, lanes_all), jnp.float32)
        for k in range(1, REACH + 1):
            near = start0 < first - jnp.float32((k - 1) * tok)
            part = part + jnp.where(near, jnp.exp(total) * en_ref[k - 1, rows, :].astype(jnp.float32), 0.0)
            total = jnp.where(near, total + dn_ref[k - 1, h : h + 1, :], total)
        begun = jnp.exp(total) * pall_ref[source, rows, :].astype(jnp.float32)
        arriving.append(part + jnp.where(inherits & (hold0 >= 0), begun, 0.0))
    arriving = jnp.concatenate(arriving, axis=0)
    high = arriving.astype(jnp.bfloat16)
    low = (arriving - high.astype(jnp.float32)).astype(jnp.bfloat16)
    c_all = jnp.concatenate([c_ref[m].astype(jnp.float32) for m in range(models)], axis=0)
    of_model = iota((lanes_all, tok), 0) // c_ref.shape[1]

    def masked(tokens, m):
        return jnp.where(tokens & (of_model == m), c_all, 0.0).astype(jnp.bfloat16)

    for m in range(models):
        c_in = masked(inherited, m)
        acc_ref[m] = jnp.dot(high, c_in, preferred_element_type=jnp.float32) + jnp.dot(
            low, c_in, preferred_element_type=jnp.float32
        )

    def borrow(r, carry):
        held = hold_s[0, r]

        @pl.when(held >= 0)
        def _():
            mine = roll_row == r.astype(jnp.float32)
            for m in range(models):
                acc_ref[m] += jnp.dot(pall_ref[held], masked(mine, m), preferred_element_type=jnp.float32)

        return carry

    lax.fori_loop(lo, hi, borrow, 0)
    for m in range(models):
        for h in range(heads):
            rows = slice(h * head, (h + 1) * head)
            gate = z_ref[m, rows, :].astype(jnp.float32)
            out = y_ref[m, rows, :] + jnp.exp(run_ref[m, h : h + 1, :]) * acc_ref[m, rows, :]
            acc_ref[m, rows, :] = out * (gate / (1.0 + jnp.exp(-gate)))
        g_ref[m] = jnp.transpose(acc_ref[m]).astype(jnp.bfloat16)


def finish_mix(len_row, lengths, holders, y, run, c, z, pall, en, dn):
    models, inner, tok = y.shape
    return pl.pallas_call(
        finish_mix_kernel,
        out_shape=jax.ShapeDtypeStruct((models, tok, inner), jnp.bfloat16),
        in_specs=[smem()] * 2 + [vmem()] * 8,
        out_specs=vmem(),
        scratch_shapes=[pltpu.VMEM((models, inner, tok), jnp.float32)],
        compiler_params=pltpu.CompilerParams(vmem_limit_bytes=VMEM_BYTES),
        cost_estimate=pl.CostEstimate(flops=10**9, bytes_accessed=8 * 10**6, transcendentals=10**6),
        name="finish_mix",
    )(lengths, holders, len_row, y, run, c, z, pall, en, dn)


def pair_ring(send, w_ref, wall_ref, oth_ref, split, own_sem):
    _, _, z, y, at_y, at_z = place()
    toward = 1 - 2 * lax.rem(y, 2)
    same, other = at_y(toward), at_y(-toward)
    y_other = lax.rem(y - toward + Y, Y)
    mine = y // 2
    rows = w_ref.shape[1]
    count = rows - split
    half = count // 32 * 16
    first, second = pl.ds(0, split), pl.ds(split, count)
    low, high = pl.ds(split, half), pl.ds(split + half, count - half)
    low_o, high_o = pl.ds(0, half), pl.ds(half, count - half)

    def zz(d):
        return lax.rem(z + d + Z, Z)

    def along(ref, peer):
        return send(ref, ref, peer)

    pending, last = [], []

    def to_y(d):
        j = zz(d)
        dst = wall_ref.at[j, y, second]
        src_same = dst if d else w_ref.at[mine, second]
        src_other = oth_ref.at[j] if d else w_ref.at[1 - mine, second]
        pending.append((j, send(src_same, dst, same), send(src_other, dst, other)))

    def pass_y():
        j, from_same, from_other = pending.pop(0)
        from_other.wait_recv()
        last.append(along(wall_ref.at[j, y_other, second], same))
        last.append(from_same)

    def along_z(d, rows_w, rows_o, peer):
        return [along(wall_ref.at[zz(d), y, rows_w], peer), along(oth_ref.at[zz(d), rows_o], peer)]

    keep = pltpu.make_async_copy(w_ref.at[mine], wall_ref.at[z, y], own_sem)
    keep.start()
    a_same = send(w_ref.at[mine, first], wall_ref.at[z, y, first], same)
    a_other = send(w_ref.at[1 - mine, first], wall_ref.at[z, y, first], other)
    right, left = (
        [
            send(w_ref.at[mine, second], wall_ref.at[z, y, second], at_z(d)),
            send(w_ref.at[1 - mine, second], oth_ref.at[z], at_z(d)),
        ]
        for d in (1, -1)
    )
    to_y(0)
    keep.wait()
    yield
    a_other.wait_recv()
    a_pass = along(wall_ref.at[z, y_other, first], same)
    a_same.wait_recv()
    yield
    a_pass.wait_recv()
    group = wall_ref.at[z, :, first]
    far_right, far_left = along(group, at_z(1)), along(group, at_z(-1))
    yield
    everything = pl.ds(0, count)
    for k in range(1, Z // 2):
        whole = k < Z // 2 - 1
        for copy in right:
            copy.wait_recv()
        right = along_z(-k, second if whole else low, everything if whole else low_o, at_z(1))
        to_y(-k)
        for copy in left:
            copy.wait_recv()
        left = along_z(k, second if whole else high, everything if whole else high_o, at_z(-1))
        to_y(k)
        yield
        pass_y()
        yield
        if k > 1:
            far_right.wait_recv()
            far_right = along(wall_ref.at[zz(1 - k), :, first], at_z(1))
            far_left.wait_recv()
            far_left = along(wall_ref.at[zz(k - 1), :, first], at_z(-1))
            yield
    for copy in right + left:
        copy.wait_recv()
    to_y(Z // 2)
    yield
    pass_y()
    pass_y()
    yield
    far_right.wait_recv()
    far_right = along(wall_ref.at[zz(1 - Z // 2), pl.ds(0, Y // 2), first], at_z(1))
    far_left.wait_recv()
    far_left = along(wall_ref.at[zz(Z // 2 - 1), pl.ds(Y // 2, Y // 2), first], at_z(-1))
    yield
    while pending:
        pass_y()
        yield
    far_right.wait_recv()
    far_left.wait_recv()
    for copy in last:
        copy.wait_recv()


PAIR_COPIES = 3 + 8 + 4 + 12 + 16 + 8


def partner_of(at_y, y):
    return at_y(2 * lax.rem(y, 2) - 1)


def finale_kernel(
    vocab,
    g_ref, wo_ref, wos_ref, dw_ref, dws_ref, up_ref, res_ref, scale_ref, head_ref,
    tgt_ref, tgp_ref, valid_ref, len_ref, owner_ref, sums_ref, delta_ref,
    gs_ref, low_ref, acc_ref, out_ref, comb_ref, relay_ref, direct_ref, sum_ref, h_ref, nall_ref, wall_ref, oth_ref,
    max_ref, exp_ref, hit_ref, want_ref, stat_ref, all_ref, part_ref, parts_ref,
    send_sem, recv_sem, ring_send, ring_recv, own_sem, s_send, s_recv, p_send, p_recv,
):
    seq, mp, z, y, at_y, at_z = place()
    x, core = mp // CORES, lax.rem(mp, CORES)
    peers, count = X * CORES, Y * Z
    chunks = acc_ref.shape[0]
    width = acc_ref.shape[4]
    share = res_ref.shape[1]
    model_width = res_ref.shape[2]
    inner = g_ref.shape[4]
    rows = X * share
    sibling = (seq, x * CORES + 1 - core)
    partner = partner_of(at_y, y)

    def xx(d):
        return lax.rem(x + d + X, X)

    def at_x(d):
        return (seq, xx(d) * CORES + core)

    barrier = pltpu.get_barrier_semaphore()
    for d in range(1, peers):
        pl.semaphore_signal(barrier, inc=1, device_id=(seq, lax.rem(mp + d, peers)), device_id_type=MESH)
    for d in range(peers):
        pl.semaphore_signal(
            barrier, inc=1, device_id=(partner[0], lax.rem(mp + d, peers)), device_id_type=MESH
        )

    def hello(d, carry):
        pl.semaphore_signal(barrier, inc=1, device_id=(lax.rem(seq + d, count), mp), device_id_type=MESH)
        return carry

    lax.fori_loop(1, count, hello, 0)
    pl.semaphore_wait(barrier, 2 * peers - 1 + count - 1)

    send, begun = make_sender(send_sem, recv_sem)
    ring_out, ring_begun = make_sender(ring_send, ring_recv)
    gated = send(g_ref.at[:, :, 1 - core], gs_ref, sibling)
    ring = pair_ring(ring_out, head_ref, wall_ref, oth_ref, PAIR_SPLIT, own_sem)

    def ring_step(times=1):
        for _ in range(times):
            next(ring, None)

    ring_step()
    own_g = g_ref[:, :, core].reshape(2 * rows, inner)
    low = jnp.dot(own_g[:rows], dw_ref[...], preferred_element_type=jnp.float32)
    gated.wait_recv()
    sib_g = gs_ref[...].reshape(2 * rows, inner)
    low = low + jnp.dot(sib_g[:rows], dws_ref[...], preferred_element_type=jnp.float32)
    low_ref[...] = low.astype(jnp.bfloat16)

    relays, directs, sums = [], [], []

    def combine(n):
        for side, d, m in ((0, 1, 0), (1, -1, 1)):
            relays[n][side].wait_recv()
            total = acc_ref[n, m, xx(d)] + relay_ref[n, side].astype(jnp.float32)
            comb_ref[n, side] = total.astype(jnp.bfloat16)
        sums.append(
            [send(comb_ref.at[n, side], sum_ref.at[n, side], at_x(d)) for side, d in ((0, 1), (1, -1))]
        )

    for n in range(chunks):
        cols = slice(n * width, (n + 1) * width)
        acc = jnp.dot(
            g_ref[:, :, core].reshape(2 * rows, inner), wo_ref[:, cols], preferred_element_type=jnp.float32
        ) + jnp.dot(gs_ref[...].reshape(2 * rows, inner), wos_ref[:, cols], preferred_element_type=jnp.float32)
        more = jnp.dot(low_ref[...], up_ref[:, cols], preferred_element_type=jnp.float32)
        acc_ref[n, 0] = (acc[:rows] + more).reshape(X, share, width)
        acc_ref[n, 1] = acc[rows:].reshape(X, share, width)
        out_ref[n] = acc_ref[n].astype(jnp.bfloat16)
        far = xx(2)
        relays.append(
            [send(out_ref.at[n, m, far], relay_ref.at[n, side], at_x(d)) for side, d, m in ((0, 1, 0), (1, -1, 1))]
        )
        directs.append(
            [
                send(out_ref.at[n, m, xx(d)], direct_ref.at[n, side], at_x(d))
                for side, d, m in ((0, 1, 1), (1, -1, 0))
            ]
        )
        if n >= 1:
            combine(n - 1)
        if n in (1, 3, 5):
            ring_step()
    combine(chunks - 1)
    ring_step()

    square = jnp.zeros((2, share, 1), jnp.float32)
    for n in range(chunks):
        cols = slice(n * width, (n + 1) * width)
        for copy in sums[n] + directs[n]:
            copy.wait_recv()
        squares = []
        for m in range(2):
            total = (
                acc_ref[n, m, x]
                + sum_ref[n, m].astype(jnp.float32)
                + direct_ref[n, 1 - m].astype(jnp.float32)
                + res_ref[m, :, cols].astype(jnp.float32)
            )
            h_ref[m, :, cols] = total
            squares.append(jnp.sum(total * total, axis=1, keepdims=True))
        square = square + jnp.stack(squares)
        if n in (1, 3, 5):
            ring_step()
    normed = (h_ref[...] * lax.rsqrt(square / model_width + 1e-05) * scale_ref[...]).astype(jnp.bfloat16)
    for m in range(2):
        nall_ref[0, m, mp] = normed[m]

    def block(p, d, m):
        return nall_ref.at[p, m, xx(d) * CORES + core]

    near, far, shared = [{}, {}], [{}, {}], []

    def near_sends(p):
        for side, d, m in ((0, 1, 0), (1, -1, 1), (0, 1, 1), (1, -1, 0)):
            near[p][side, m] = send(block(p, 0, m), block(p, 0, m), at_x(d))
        for m in range(2):
            shared.append(send(block(p, 0, m), block(p, 0, m), sibling))

    def far_sends(p):
        for side, d, m in ((0, 1, 0), (1, -1, 1)):
            near[p][side, m].wait_recv()
            far[p][side] = send(block(p, -d, m), block(p, -d, m), at_x(d))
            shared.append(send(block(p, -d, m), block(p, -d, m), sibling))

    def rest(p):
        for side, d, m in ((0, 1, 1), (1, -1, 0)):
            near[p][side, m].wait_recv()
            shared.append(send(block(p, -d, m), block(p, -d, m), sibling))

    def beyond(p):
        for side, m in ((0, 0), (1, 1)):
            far[p][side].wait_recv()
            shared.append(send(block(p, 2, m), block(p, 2, m), sibling))

    to_partner = [send(block(0, 0, m), nall_ref.at[1, m, mp], partner) for m in range(2)]
    near_sends(0)
    ring_step()
    far_sends(0)
    ring_step()
    for copy in to_partner:
        copy.wait_recv()
    near_sends(1)
    rest(0)
    ring_step()
    beyond(0)
    ring_step()
    far_sends(1)
    ring_step()
    rest(1)
    ring_step()
    beyond(1)
    eye = (iota((rows * 2, rows * 2), 0) == iota((rows * 2, rows * 2), 1)).astype(jnp.float32)
    for p, ref in ((0, tgt_ref), (1, tgp_ref)):
        column = lax.dot_general(
            eye, ref[...], (((1,), (1,)), ((), ())), precision=HIGHEST, preferred_element_type=jnp.float32
        )[:, 0:1]
        want_ref[p, 0 : rows * 2, :] = column
        want_ref[p, rows * 2 : rows * 4, :] = column
    max_ref[...] = jnp.full(max_ref.shape, -3e38, jnp.float32)
    exp_ref[...] = jnp.zeros(exp_ref.shape, jnp.float32)
    hit_ref[...] = jnp.zeros(hit_ref.shape, jnp.float32)
    for _ in ring:
        pass
    for copy in shared:
        copy.wait_recv()

    tiles = wall_ref.shape[3] // TILE
    depth = wall_ref.shape[0] * wall_ref.shape[1] * wall_ref.shape[2]
    base = (y // 2) * wall_ref.shape[3]
    all_rows = rows * 4

    def score(i, carry):
        p, j = i // tiles, lax.rem(i, tiles)
        cols = pl.ds(pl.multiple_of(j * TILE, TILE), TILE)
        logits = jnp.dot(
            nall_ref[p].reshape(all_rows, depth), wall_ref[:, :, :, cols].reshape(depth, TILE),
            preferred_element_type=jnp.float32,
        )
        col = iota((all_rows, TILE), 1) + (base + j * TILE)
        real = col < vocab
        wanted = col.astype(jnp.float32) + jnp.float32(1) * (mp * vocab) == want_ref[p]
        logits = jnp.where(real, logits, -3e38)
        top = jnp.maximum(max_ref[p], jnp.max(logits, axis=1, keepdims=True))
        exp_ref[p] = exp_ref[p] * jnp.exp(max_ref[p] - top) + jnp.sum(
            jnp.where(real, jnp.exp(logits - top), 0.0), axis=1, keepdims=True
        )
        max_ref[p] = top
        hit_ref[p] += jnp.sum(jnp.where(real & wanted, logits, 0.0), axis=1, keepdims=True)
        return carry

    lax.fori_loop(0, 2 * tiles, score, 0)
    lane = iota((all_rows, 128), 1)
    for p in range(2):
        packed = jnp.where(
            lane == 0, max_ref[p], jnp.where(lane == 1, exp_ref[p], jnp.where(lane == 2, hit_ref[p], 0.0))
        )
        stat_ref[p] = jnp.transpose(packed)[0:8]

    def stats(p, d):
        return pltpu.make_async_remote_copy(
            src_ref=stat_ref.at[p], dst_ref=all_ref.at[p, mp], send_sem=s_send.at[p, d], recv_sem=s_recv.at[p, d],
            device_id=(partner[0] if p else seq, lax.rem(mp + d, peers)), device_id_type=MESH,
        )

    exchange = [(1, d) for d in range(peers)] + [(0, d) for d in range(1, peers)]
    for p, d in exchange:
        stats(p, d).start()
    all_ref[0, mp] = stat_ref[0]
    tok = valid_ref.shape[1]
    starts_row, roll_col, _, _ = rollout_tables(len_ref[...].astype(jnp.float32), seq * tok, tok)
    lanes = starts_row.shape[1]
    member = (roll_col == iota((tok, lanes), 1).astype(jnp.float32)).astype(jnp.float32)
    for copy in begun + ring_begun:
        copy.wait_send()
    for p, d in exchange:
        stats(p, d).wait_recv()
    found = [all_ref[p, k] for p in range(2) for k in range(peers)]
    top = functools.reduce(jnp.maximum, [f[0:1] for f in found])
    total = functools.reduce(jnp.add, [f[1:2] * jnp.exp(f[0:1] - top) for f in found])
    hit = functools.reduce(jnp.add, [f[2:3] for f in found])
    logprob = hit - top - jnp.log(total)
    delta = (logprob[:, :tok] - logprob[:, tok:]) * valid_ref[...].astype(jnp.float32)
    delta_ref[...] = delta
    part_ref[...] = jnp.dot(
        jnp.broadcast_to(delta, (8, tok)), member, precision=HIGHEST, preferred_element_type=jnp.float32
    )

    def parts(d):
        return pltpu.make_async_remote_copy(
            src_ref=part_ref, dst_ref=parts_ref.at[seq], send_sem=p_send.at[d], recv_sem=p_recv.at[d],
            device_id=(lax.rem(seq + d, count), mp), device_id_type=MESH,
        )

    def begin(d, carry):
        parts(d).start()
        return carry

    def end(d, carry):
        parts(d).wait_recv()
        return carry

    def drain(d, carry):
        parts(d).wait_send()
        return carry

    lax.fori_loop(1, count, begin, 0)
    parts_ref[seq] = part_ref[...]
    for p, d in exchange:
        stats(p, d).wait_send()
    lax.fori_loop(1, count, end, 0)
    means = functools.reduce(jnp.add, [parts_ref[k] for k in range(count)])[0:1] / len_ref[...].astype(jnp.float32)
    sums_ref[...] = jnp.where(owner_ref[...] == seq, means, 0.0)[:, : sums_ref.shape[1]]
    lax.fori_loop(1, count, drain, 0)


def finale(vocab, gated, wo, wos, dw, dws, up, res, scale, head, tgt, tgp, valid_row, len_row, owner_row, rolls):
    models, tok, inner = gated.shape
    width_all = wo.shape[1]
    share = res.shape[1]
    width = 512
    chunks = width_all // width
    bf16, f32 = jnp.bfloat16, jnp.float32
    dma = pltpu.SemaphoreType.DMA
    copies = 1 + 6 * chunks + 2 + 2 * 14
    peers, count = X * CORES, Y * Z
    piece = pltpu.VMEM((chunks, 2, share, width), bf16)
    column = pltpu.VMEM((2, models * tok, 1), f32)
    _, head_rows, head_cols = head.shape
    lanes = len_row.shape[1]
    return pl.pallas_call(
        functools.partial(finale_kernel, vocab),
        out_shape=(jax.ShapeDtypeStruct((1, rolls), f32), jax.ShapeDtypeStruct((1, tok), f32)),
        in_specs=[vmem()] * 8 + [anywhere()] + [vmem()] * 5,
        out_specs=(vmem(),) * 2,
        scratch_shapes=[
            pltpu.VMEM((models, X, share, inner), bf16),
            pltpu.VMEM((X * share, dw.shape[1]), bf16),
            pltpu.VMEM((chunks, models, X, share, width), f32),
            pltpu.VMEM((chunks, models, X, share, width), bf16),
            piece, piece, piece, piece,
            pltpu.VMEM((models, share, width_all), f32),
            pltpu.VMEM((2, models, peers, share, width_all), bf16),
            pltpu.VMEM((Z, Y, head_rows, head_cols), bf16),
            pltpu.VMEM((Z, head_rows - PAIR_SPLIT, head_cols), bf16),
            column, column, column, column,
            pltpu.VMEM((2, 8, models * tok), f32),
            pltpu.VMEM((2, peers, 8, models * tok), f32),
            pltpu.VMEM((8, lanes), f32),
            pltpu.VMEM((count, 8, lanes), f32),
            dma((copies,)), dma((copies,)), dma((PAIR_COPIES,)), dma((PAIR_COPIES,)), dma,
            dma((2, peers)), dma((2, peers)), dma((count,)), dma((count,)),
        ],
        compiler_params=pltpu.CompilerParams(
            collective_id=2, has_side_effects=True, vmem_limit_bytes=VMEM_BYTES
        ),
        cost_estimate=pl.CostEstimate(flops=2 * 10**10, bytes_accessed=10**8, transcendentals=10**6),
        name="finale",
    )(
        gated.reshape(models, X, CORES, share, inner), wo, wos, dw, dws, up, res, scale, head,
        tgt, tgp, valid_row, len_row, owner_row,
    )


def shards(
    scored_token_targets, valid, lengths, owners, holders, mixer_input_x, mixer_gate_input,
    input_projection_b, output_projection_c, token_step_sizes, head_decay_rate, head_skip_scale,
    prompt_held_states, shared_output_weight, adapter_down_weight, adapter_up_weight,
    residual, final_norm_scale, vocab_head_weight,
):
    tok = scored_token_targets.shape[0]
    models, _, inner = mixer_input_x.shape
    state = input_projection_b.shape[2]
    rolls = lengths.shape[0]
    share = tok // (X * CORES)
    mp = lax.axis_index("mp")
    vocab = vocab_head_weight.shape[1]
    half = -(-vocab // (2 * TILE)) * TILE
    head = jnp.stack(
        [vocab_head_weight[:, :half], jnp.pad(vocab_head_weight[:, half:], ((0, 0), (0, 2 * half - vocab)))]
    )
    target = jnp.broadcast_to(scored_token_targets.astype(jnp.float32)[None, :], (8, tok))

    def row(values, fill):
        return jnp.pad(values, (0, 128 - rolls), constant_values=fill)[None, :]

    len_row, owner_row = row(lengths, 0), row(owners, -1)
    prompts = jnp.transpose(prompt_held_states[:, 0], (1, 2, 0, 3)).reshape(inner, models * state)
    own_res = jnp.transpose(lax.dynamic_slice_in_dim(residual, mp * share, share, 0), (1, 0, 2))
    x, b, c, z = (
        jnp.swapaxes(a, 1, 2)
        for a in (mixer_input_x, input_projection_b, output_projection_c, mixer_gate_input)
    )
    y, run, ends, last = local_mix(
        len_row, x, b, c, jnp.transpose(token_step_sizes, (2, 0, 1)), head_decay_rate, head_skip_scale
    )
    pall, en, dn, wos, dws, target_p = states(
        prompts, ends, last, shared_output_weight, adapter_down_weight, target
    )
    gated = finish_mix(
        len_row, lengths[None, :], holders[None, :], y, run, c, z,
        pall.reshape((Z * Y,) + prompts.shape), en, dn,
    )
    sums, delta = finale(
        vocab, gated, shared_output_weight, wos, adapter_down_weight, dws, adapter_up_weight, own_res,
        final_norm_scale[None, :], head, target, target_p, valid[None, :], len_row, owner_row, rolls,
    )
    return sums, delta.reshape(tok)


def solution(mesh):
    placed = (
        P("seq"), P("seq"), P(), P(), P(),
        P(None, "seq", "mp"), P(None, "seq", "mp"),
        P(None, "seq", None), P(None, "seq", None), P(None, "seq", "mp"),
        P(None, "mp"), P(None, "mp"), P(None, "seq", "mp", None, None),
        P("mp", None), P("mp", None), P(), P("seq", None, None), P(), P("seq", "mp"),
    )
    return jax.shard_map(
        shards, mesh=mesh, in_specs=placed, out_specs=(P("seq", None), P("seq")), check_vma=False
    )
```
